256 devices in a mesh: row: 16 (over z, y_lo), col: 16 (over x, y_hi, core).
Axes of the slice: x: 4, y: 4 (y_hi: 2, y_lo: 2; y = y_hi * 2 + y_lo), z: 8, core: 2. Of those that a mesh axis runs over, the one named last changes fastest.
Arguments:
- velocity: float32 [3, 128, 256, 1024], P(None, 'col', 'row'), may hold values from -6 to 6
- derivative_x: float32 [1024, 1024], replicated, may hold values from -4 to 4, as said below
- derivative_y: float32 [256, 256], replicated, may hold values from -4 to 4, as said below
- derivative_z: float32 [128, 128], replicated, may hold values from -4 to 4, as said below
- smoothing_x: float32 [1024, 1024], replicated, may hold values from -2 to 2, as said below
- smoothing_y: float32 [256, 256], replicated, may hold values from -2 to 2, as said below
- smoothing_z: float32 [128, 128], replicated, may hold values from -2 to 2, as said below
Outputs:
- filtered_velocity: float32 [3, 128, 256, 1024], P(None, 'col', 'row')
The draws below stay inside these ranges and needn't reach their ends.
Inputs may be any that keep to these rules, and one draw needn't show every extreme that they name: derivative_x is diag(m) times the inverse of the periodic tridiagonal matrix with 1 on the diagonal and 9/20 beside it, times the periodic stencil 63/80 (f[i+1] - f[i-1]) + 9/100 (f[i+2] - f[i-2]) - 7/1200 (f[i+3] - f[i-3]); m holds one positive metric factor per grid line. `derivative_y`: as derivative_x, for the y lines. smoothing_x is the inverse of the periodic tridiagonal matrix with 1 on the diagonal and a[i] beside it in row i, times the periodic filter stencil of row i, whose weights are: at offset 0, 11/16 plus 5/8 times a[i]; at offsets -1 and 1 each, 15/64 plus 17/32 times a[i]; at offsets -2 and 2 each, -3/32 plus 3/16 times a[i]; at offsets -3 and 3 each, 1/64 minus 1/32 times a[i]; each a[i] lies in 0.44 to 0.499. `derivative_z`: as derivative_x, for the z lines. `smoothing_y`: as smoothing_x, for the y lines. `smoothing_z`: as smoothing_x, for the z lines.
All inputs are finite; a program needn't handle non-finite values.
Results may differ from the reference program's by a relative error of at most 0.000082.
Values sent between devices are 32-bit elements; how exact they have to be, the bound alone decides.
A program may use at most 64 MiB of HBM per device.

```python
import math
import jax
import jax.numpy as jnp
from jax import lax

NX = 1024
NY = 256
NZ = 128


def shifted_eye(count, offset):
    return jnp.roll(jnp.eye(count, dtype=jnp.float32), offset, axis=1)


def pade_matrix(key, count):
    metric = jnp.exp(jax.random.uniform(key, (count,), jnp.float32, math.log(0.6), math.log(1.6)))
    left = jnp.eye(count, dtype=jnp.float32) + (shifted_eye(count, 1) + shifted_eye(count, -1)) * (9.0 / 20.0)
    right = 63.0 / 80.0 * (shifted_eye(count, 1) - shifted_eye(count, -1))
    right = right + 9.0 / 100.0 * (shifted_eye(count, 2) - shifted_eye(count, -2))
    right = right - 7.0 / 1200.0 * (shifted_eye(count, 3) - shifted_eye(count, -3))
    return metric[:, None] * jnp.linalg.solve(left, right)


def filter_matrix(key, count):
    alpha = jax.random.uniform(key, (count,), jnp.float32, 0.44, 0.495)
    coef_zero = (11.0 + 10.0 * alpha) / 16.0
    coef_one = (15.0 + 34.0 * alpha) / 64.0
    coef_two = (-3.0 + 6.0 * alpha) / 32.0
    coef_three = (1.0 - 2.0 * alpha) / 64.0
    left = jnp.eye(count, dtype=jnp.float32) + alpha[:, None] * (shifted_eye(count, 1) + shifted_eye(count, -1))
    right = coef_zero[:, None] * jnp.eye(count, dtype=jnp.float32)
    right = right + coef_one[:, None] * (shifted_eye(count, 1) + shifted_eye(count, -1))
    right = right + coef_two[:, None] * (shifted_eye(count, 2) + shifted_eye(count, -2))
    right = right + coef_three[:, None] * (shifted_eye(count, 3) + shifted_eye(count, -3))
    return jnp.linalg.solve(left, right)


def draw_derivative_x(key, part):
    return pade_matrix(jax.random.fold_in(key, 11), NX)


def draw_derivative_y(key, part):
    return pade_matrix(jax.random.fold_in(key, 12), NY)


def draw_derivative_z(key, part):
    return pade_matrix(jax.random.fold_in(key, 13), NZ)


def draw_smoothing_x(key, part):
    return filter_matrix(jax.random.fold_in(key, 21), NX)


def draw_smoothing_y(key, part):
    return filter_matrix(jax.random.fold_in(key, 22), NY)


def draw_smoothing_z(key, part):
    return filter_matrix(jax.random.fold_in(key, 23), NZ)


def block_levels(own_key, shape, split, least, top_value):
    def one(axis_at, shards_of):
        draws = jax.random.uniform(jax.random.fold_in(jax.random.fold_in(own_key, 6), axis_at), (shards_of,), jnp.float32, least / len(split), top_value / len(split))
        return jnp.repeat(jnp.exp(draws), shape[axis_at] // shards_of).reshape((-1,) + (1,) * (len(shape) - axis_at - 1))

    loudness = one(*split[0])
    for cut in split[1:]:
        loudness = loudness * one(*cut)
    return loudness


def noise(key, dims, width, reach, shards=(), kind=jnp.bfloat16):
    entries = width * jax.random.normal(key, dims, jnp.float32)
    if shards:
        entries = entries * block_levels(key, dims, shards, -0.22, 0.18)
    return jnp.clip(entries, -reach, reach).astype(kind)


def setup_inputs(seed: int = 0) -> dict:
    arg_keys = jax.random.split(jax.random.key(seed), 8)
    velocity = noise(arg_keys[0], (3, NZ, NY, NX), 1.0, 6.0, ((1, 16), (2, 16)), jnp.float32)
    derivative_x = draw_derivative_x(jax.random.fold_in(arg_keys[7], 71), 0)
    derivative_y = draw_derivative_y(jax.random.fold_in(arg_keys[7], 71), 0)
    derivative_z = draw_derivative_z(jax.random.fold_in(arg_keys[7], 71), 0)
    smoothing_x = draw_smoothing_x(jax.random.fold_in(arg_keys[7], 71), 0)
    smoothing_y = draw_smoothing_y(jax.random.fold_in(arg_keys[7], 71), 0)
    smoothing_z = draw_smoothing_z(jax.random.fold_in(arg_keys[7], 71), 0)
    return {"velocity": velocity, "derivative_x": derivative_x, "derivative_y": derivative_y, "derivative_z": derivative_z, "smoothing_x": smoothing_x, "smoothing_y": smoothing_y, "smoothing_z": smoothing_z}


def apply_x(matrix, field):
    return jnp.einsum('xk,czyk->czyx', matrix, field, precision=lax.Precision.HIGHEST)

def apply_y(matrix, field):
    return jnp.einsum('yk,czkx->czyx', matrix, field, precision=lax.Precision.HIGHEST)

def apply_z(matrix, field):
    return jnp.einsum('zk,ckyx->czyx', matrix, field, precision=lax.Precision.HIGHEST)

def reference(velocity, derivative_x, derivative_y, derivative_z, smoothing_x, smoothing_y, smoothing_z):
    tendency = -(apply_x(derivative_x, velocity * velocity[0:1]) + apply_y(derivative_y, velocity * velocity[1:2]) + apply_z(derivative_z, velocity * velocity[2:3]))
    advanced = velocity + 0.1 * tendency
    smooth = apply_y(smoothing_y, advanced)
    smooth = apply_z(smoothing_z, smooth)
    return apply_x(smoothing_x, smooth)
```

```python
import functools

import jax
import jax.numpy as jnp
import numpy as np
from jax import lax
from jax.experimental import pallas as pl
from jax.experimental.pallas import tpu as pltpu
from jax.sharding import Mesh
from jax.sharding import PartitionSpec as P

AXES = ("z", "ylo", "x", "yhi", "core")
SIZES = (8, 2, 4, 2, 2)
MESH = pl.DeviceIdType.MESH
HIGHEST = lax.Precision.HIGHEST
F32 = jnp.float32
BLK = 32
NBY, NBZ, NBX = 8, 4, 8
ORDER = (1, 2, 0)
SIDE = 9.0 / 20.0
STENCIL = (63.0 / 80.0, 9.0 / 100.0, -7.0 / 1200.0)


def tridiagonal_tables(side, count):
    piv, cp = np.zeros(count), np.zeros(count)
    before = 0.0
    for i in range(count):
        piv[i] = 1.0 / (1.0 - side * before)
        before = cp[i] = side * piv[i]
    first, last = np.zeros(count), np.zeros(count)
    first[0] = cp[0]
    for i in range(1, count):
        first[i] = -cp[i] * first[i - 1]
    last[-1] = cp[-1]
    for i in range(count - 2, -1, -1):
        first[i] -= cp[i] * first[i + 1]
        last[i] = -cp[i] * last[i + 1]
    return np.stack([piv, cp, first, last])


def reduced_inverse(table, blocks):
    first, last = table[2], table[3]
    full = np.eye(16)
    for i in range(blocks):
        before, after = 8 + (i - 1) % blocks, (i + 1) % blocks
        full[i, before] += first[0]
        full[i, after] += last[0]
        full[8 + i, before] += first[-1]
        full[8 + i, after] += last[-1]
    return np.linalg.inv(full)


def lanes(array):
    return np.broadcast_to(np.asarray(array, np.float32)[..., None], array.shape + (128,))


def pade_off_diagonal(count):
    left = np.eye(count) + SIDE * (np.roll(np.eye(count), 1, 1) + np.roll(np.eye(count), -1, 1))
    right = sum(
        w * (np.roll(np.eye(count), k + 1, 1) - np.roll(np.eye(count), -k - 1, 1))
        for k, w in enumerate(STENCIL)
    )
    return float(np.linalg.solve(left, right)[0, 1])


def outside_profile():
    inner = 122
    matrix = np.eye(inner) + SIDE * (np.eye(inner, k=1) + np.eye(inner, k=-1))
    profile = np.zeros((8, 128))
    for e, row in enumerate((0, 1, 2, 125, 126, 127)):
        profile[e, row] = 1.0
    unit = np.zeros(inner)
    unit[0] = -SIDE
    profile[2, 3:125] = np.linalg.solve(matrix, unit)
    profile[3, 3:125] = np.linalg.solve(matrix, unit[::-1])
    return profile


def iota(shape, dim):
    return lax.broadcasted_iota(jnp.int32, shape, dim)


def wrapped_offset(shape, first_row, count):
    offset = iota(shape, 1) - iota(shape, 0) - first_row
    return jnp.where(offset < 0, offset + count, offset)


def metric_rows(matrix_ref, first_row, count, unit):
    block = matrix_ref[pl.ds(first_row, BLK), :]
    offset = wrapped_offset(block.shape, first_row, count)
    weight = jnp.where(offset == 1, 0.5 / unit, jnp.where(offset == count - 1, -0.5 / unit, 0.0))
    return jnp.broadcast_to(jnp.sum(block * weight, axis=1, keepdims=True), (BLK, 128))


def filter_slack(matrix_ref, count):
    shape = (count, count)
    offset = wrapped_offset(shape, 0, count)
    change = matrix_ref[...] - jnp.where(offset == 0, 1.0, 0.0)
    around = 0.5 * (pltpu.roll(change, 1, 0) + pltpu.roll(change, count - 1, 0))
    sixth = jnp.zeros(shape, F32)
    for k, w in enumerate((-20.0, 15.0, -6.0, 1.0)):
        sixth = jnp.where((offset == k) | (offset == (count - k) % count), w / 64.0, sixth)
    basis = sixth + around
    top = jnp.sum((change + around) * basis, axis=1, keepdims=True)
    return top / jnp.sum(basis * basis, axis=1, keepdims=True)


def block_tables(slack_ref, all_ref):
    def side(i):
        return 0.5 - 0.5 * slack_ref[pl.ds(i, 8, stride=BLK), :]

    def forward(i, carry):
        before, first = carry
        a = side(i)
        piv = 1.0 / (1.0 - a * before)
        cp = a * piv
        first = jnp.where(i == 0, cp, -cp * first)
        all_ref[0, i] = piv
        all_ref[1, i] = cp
        all_ref[2, i] = first
        return cp, first

    zero = jnp.zeros((8, 128), F32)
    lax.fori_loop(0, BLK, forward, (zero, zero))

    def backward(k, carry):
        first, last = carry
        i = BLK - 1 - k
        cp = all_ref[1, i]
        first = all_ref[2, i] - cp * first
        last = jnp.where(k == 0, cp, -cp * last)
        all_ref[2, i] = first
        all_ref[3, i] = last
        return first, last

    lax.fori_loop(0, BLK, backward, (zero, zero))


def invert_reduced(all_ref, blocks, out_ref):
    sub, lane = iota((8, 128), 0), iota((8, 128), 1)
    before = 8 + jnp.where(sub == 0, blocks - 1, sub - 1)
    after = jnp.where(sub == blocks - 1, 0, sub + 1)
    valid = sub < blocks

    def rows(own, first, last):
        value = jnp.where(lane == own, 1.0, 0.0)
        value += jnp.where(valid & (lane == before), first, 0.0)
        return value + jnp.where(valid & (lane == after), last, 0.0)

    full = jnp.concatenate(
        [
            rows(sub, all_ref[2, 0], all_ref[3, 0]),
            rows(8 + sub, all_ref[2, BLK - 1], all_ref[3, BLK - 1]),
        ],
        axis=0,
    )
    sub, lane = iota((16, 128), 0), iota((16, 128), 1)
    full += jnp.where(lane == 16 + sub, 1.0, 0.0)

    def eliminate(k, full):
        column = jnp.sum(jnp.where(lane == k, full, 0.0), axis=1, keepdims=True)
        row = jnp.sum(jnp.where(sub == k, full, 0.0), axis=0, keepdims=True)
        pivot = jnp.sum(jnp.where(sub == k, column, 0.0), axis=0, keepdims=True)[:, :1]
        row = row / pivot
        return jnp.where(sub == k, row, full - column * row)

    full = lax.fori_loop(0, 16, eliminate, full)

    def spread(k, carry):
        column = jnp.sum(jnp.where(lane == 16 + k, full, 0.0), axis=1, keepdims=True)
        out_ref[k] = jnp.broadcast_to(column, (16, 128))
        return carry

    lax.fori_loop(0, 16, spread, 0)


def solve_lines(rhs, table_ref, out_ref):
    def forward(i, before):
        value = rhs(i) * table_ref[0, pl.ds(i, 1), :] - table_ref[1, pl.ds(i, 1), :] * before
        out_ref[i] = value
        return value

    last = lax.fori_loop(0, BLK, forward, jnp.zeros((BLK, 128), F32))

    def backward(k, after):
        i = BLK - 2 - k
        value = out_ref[i] - table_ref[1, pl.ds(i, 1), :] * after
        out_ref[i] = value
        return value

    lax.fori_loop(0, BLK - 1, backward, last)


def derivative_rhs(field):
    def rhs(i):
        total = STENCIL[0] * (field[i + 4] - field[i + 2])
        total += STENCIL[1] * (field[i + 5] - field[i + 1])
        return total + STENCIL[2] * (field[i + 6] - field[i])

    return rhs


def filter_rhs(field, slack_ref, first_row):
    def rhs(i):
        total = (field[i] + field[i + 6]) - 6.0 * (field[i + 1] + field[i + 5])
        total += 15.0 * (field[i + 2] + field[i + 4]) - 20.0 * field[i + 3]
        return total * (slack_ref[pl.ds(first_row + i, 1), :] * (1.0 / 64.0))

    return rhs


def kernel(
    u,
    dx,
    dy,
    dz,
    sy,
    sz,
    const_table,
    const_ry,
    const_rz,
    const_profile,
    home,
    uz,
    uy,
    prod,
    gz,
    gy,
    w0,
    wy,
    vy,
    wz,
    vz,
    out,
    es,
    er,
    dxb,
    dtop,
    dbot,
    hm,
    wprof,
    slack_y,
    slack_z,
    all_y,
    all_z,
    tab_y,
    tab_z,
    met_y,
    met_z,
    ry,
    rz,
    zz,
    yz,
    yin,
    yout,
    yback,
    dma,
    loc,
    tin_s,
    tin_r,
    es_s,
    es_r,
    halo_s,
    halo_r,
    zz_s,
    zz_r,
    ya_s,
    ya_r,
    yb_s,
    yb_r,
    tout_s,
    tout_r,
):
    z, x = lax.axis_index("z"), lax.axis_index("x")
    ylo, yhi, core = lax.axis_index("ylo"), lax.axis_index("yhi"), lax.axis_index("core")
    me = (yhi * 2 + ylo) * 2 + core

    def flip(index, bit):
        return 1 - index if bit else index

    def partner(k):
        return {"yhi": flip(yhi, k >> 2), "ylo": flip(ylo, (k >> 1) & 1), "core": flip(core, k & 1)}

    def number(d):
        return (d["yhi"] * 2 + d["ylo"]) * 2 + d["core"]

    def x_lanes(g):
        return pl.ds(pl.multiple_of(g * 128, 128), 128)

    def z_rows(d):
        return pl.multiple_of((d["yhi"] * 2 + d["core"]) * 8, 8)

    def y_rows(d):
        return pl.multiple_of(d["ylo"] * 16, 16)

    here = {"yhi": yhi, "ylo": ylo, "core": core}
    remote = functools.partial(pltpu.make_async_remote_copy, device_id_type=MESH)

    greeted = [partner(k) for k in range(1, 8)]
    greeted += [{"x": lax.rem(x + k, NBZ)} for k in range(1, NBZ)]
    greeted += [{"z": lax.rem(z + k, NBY)} for k in range(1, NBY)]
    barrier = pltpu.get_barrier_semaphore()
    for d in greeted:
        pl.semaphore_signal(barrier, inc=1, device_id=d, device_id_type=MESH)
    pl.semaphore_wait(barrier, len(greeted))

    def exchange_in(c, k):
        d = partner(k)
        return remote(
            src_ref=u.at[c, :, :, x_lanes(number(d))],
            dst_ref=uz.at[c, pl.ds(3 + z_rows(here), 8), pl.ds(y_rows(here), 16), :],
            send_sem=tin_s.at[c, k],
            recv_sem=tin_r.at[c, k],
            device_id=d,
        )

    def keep_in(c):
        return pltpu.make_async_copy(
            u.at[c, :, :, x_lanes(me)],
            uz.at[c, pl.ds(3 + z_rows(here), 8), pl.ds(y_rows(here), 16), :],
            loc.at[c],
        )

    for c in ORDER:
        for k in range(1, 8):
            exchange_in(c, k).start()
        keep_in(c).start()

    first_x = pl.multiple_of(me * 128, 128)
    loads = [
        pltpu.make_async_copy(dx.at[pl.ds(first_x, 128), pl.ds(first_x, 128)], dxb, dma.at[0])
    ]
    for b in range(NBX):
        loads.append(
            pltpu.make_async_copy(dx.at[pl.ds(b * 128, 8), :], dtop.at[b], dma.at[1 + b])
        )
        loads.append(
            pltpu.make_async_copy(dx.at[pl.ds(b * 128 + 120, 8), :], dbot.at[b], dma.at[9 + b])
        )
    for load in loads:
        load.start()
    for load in loads:
        load.wait()

    column_block = iota((8, 1024), 1) // 128
    for b in range(NBX):
        rows = jnp.concatenate([dtop[b, 0:3], dbot[b, 5:8], jnp.zeros((2, 1024), F32)], axis=0)
        hm[pl.ds(b * 8, 8), :] = jnp.where(column_block == b, 0.0, rows)
    for c in range(3):
        product = (u[c] * u[0]).reshape(128, 1024)
        value = lax.dot_general(
            hm[...],
            product,
            (((1,), (1,)), ((), ())),
            precision=HIGHEST,
            preferred_element_type=F32,
        )
        es[:, c] = value.reshape(NBX, 8, 128)

    def exchange_extra(k):
        d = partner(k)
        return remote(
            src_ref=es.at[number(d)],
            dst_ref=er.at[me],
            send_sem=es_s.at[k],
            recv_sem=es_r.at[k],
            device_id=d,
        )

    for k in range(1, 8):
        exchange_extra(k).start()
    er[me] = es[me]

    first_y = pl.multiple_of(z * BLK, BLK)
    first_z = pl.multiple_of(x * BLK, BLK)
    met_y[...] = metric_rows(dy, first_y, 256, pade_off_diagonal(256))
    met_z[...] = metric_rows(dz, first_z, 128, pade_off_diagonal(128))
    slack_y[...] = jnp.broadcast_to(filter_slack(sy, 256), (256, 128))
    half = jnp.broadcast_to(filter_slack(sz, 128), (128, 128))
    slack_z[0:128, :] = half
    slack_z[128:256, :] = half
    block_tables(slack_y, all_y)
    block_tables(slack_z, all_z)

    def pick(i, carry):
        for t in range(4):
            tab_y[t, pl.ds(i, 1), :] = all_y[t, i, pl.ds(z, 1), :]
            tab_z[t, pl.ds(i, 1), :] = all_z[t, i, pl.ds(x, 1), :]
        return carry

    lax.fori_loop(0, BLK, pick, 0)
    invert_reduced(all_y, NBY, ry)
    invert_reduced(all_z, NBZ, rz)

    unit_x = pade_off_diagonal(1024)
    row, col = iota((128, 128), 0), iota((128, 128), 1)
    ends = jnp.where((row == 0) | (row == 127), 1.0 / unit_x, 0.5 / unit_x)
    weight = jnp.where(col == row + 1, ends, jnp.where(col == row - 1, -ends, 0.0))
    metric = lax.dot_general(
        jnp.ones((8, 128), F32),
        dxb[...] * weight,
        (((1,), (1,)), ((), ())),
        precision=HIGHEST,
        preferred_element_type=F32,
    )
    lane, sub = iota((8, 128), 1), iota((8, 128), 0)

    def metric_at(i):
        return jnp.sum(jnp.where(lane == i, metric, 0.0), axis=1, keepdims=True)

    single = (lane < 3) | (lane > 124)
    at_end = jnp.where(sub == 2, metric_at(2), metric_at(125))
    wprof[...] = const_profile[...] * jnp.where(single, 1.0, metric / at_end)

    def halo(stage, c, field, axis, size, side):
        index = {"z": z, "x": x}[axis]
        if side == 0:
            src, dst, to = 32, 0, lax.rem(index + 1, size)
        else:
            src, dst, to = 3, 35, lax.rem(index + size - 1, size)
        return remote(
            src_ref=field.at[c, pl.ds(src, 3)],
            dst_ref=field.at[c, pl.ds(dst, 3)],
            send_sem=halo_s.at[stage, c, side],
            recv_sem=halo_r.at[stage, c, side],
            device_id={axis: to},
        )

    halos = {
        0: functools.partial(halo, 0, field=uz, axis="x", size=NBZ),
        1: functools.partial(halo, 1, field=uy, axis="z", size=NBY),
        2: functools.partial(halo, 2, field=wy, axis="z", size=NBY),
        3: functools.partial(halo, 3, field=wz, axis="x", size=NBZ),
    }

    def start_halo(stage, c):
        for side in range(2):
            halos[stage](c=c, side=side).start()

    def wait_halo(stage, c):
        for side in range(2):
            halos[stage](c=c, side=side).wait_recv()

    def z_ends(op, c, k):
        return remote(
            src_ref=zz.at[op, c, x],
            dst_ref=zz.at[op, c, x],
            send_sem=zz_s.at[op, c, k],
            recv_sem=zz_r.at[op, c, k],
            device_id={"x": lax.rem(x + k, NBZ)},
        )

    def start_z_ends(op, c, solved):
        zz[op, c, x, 0] = solved[c, 0]
        zz[op, c, x, 1] = solved[c, BLK - 1]
        for k in range(1, NBZ):
            z_ends(op, c, k).start()

    def z_neighbours(op, c, inverse):
        for k in range(1, NBZ):
            z_ends(op, c, k).wait_recv()
        values = []
        for target in (8 + lax.rem(x + NBZ - 1, NBZ), lax.rem(x + 1, NBZ)):
            total = None
            for j in range(NBZ):
                for end in range(2):
                    term = inverse[8 * end + j, pl.ds(target, 1), :] * zz[op, c, j, end]
                    total = term if total is None else total + term
            values.append(total)
        return values

    def y_ends(op, c, t):
        return remote(
            src_ref=yz.at[op, c, :, pl.ds(8 * t, 8), :],
            dst_ref=yin.at[op, c, z],
            send_sem=ya_s.at[op, c, t],
            recv_sem=ya_r.at[op, c, z],
            device_id={"z": (4 * c + t) % NBY},
        )

    def start_y_ends(op, c, solved):
        yz[op, c, 0] = solved[c, 0]
        yz[op, c, 1] = solved[c, BLK - 1]
        for t in range(4):
            solver = (4 * c + t) % NBY

            @pl.when(z != solver)
            def _():
                y_ends(op, c, t).start()

            @pl.when(z == solver)
            def _():
                yin[op, c, z] = yz[op, c, :, 8 * t : 8 * t + 8, :]

    def y_answer(op, c, part, i):
        return remote(
            src_ref=yout.at[op, c, i],
            dst_ref=yback.at[op, c, :, pl.ds(pl.multiple_of(part * 8, 8), 8), :],
            send_sem=yb_s.at[op, c, i],
            recv_sem=yb_r.at[op, c, part],
            device_id={"z": i},
        )

    def solve_y_ends(op, c, inverse):
        part = lax.rem(z + NBY - (4 * c) % NBY, NBY)

        @pl.when(part < 4)
        def _():
            for j in range(NBY):

                @pl.when(z != j)
                def _():
                    remote(
                        src_ref=yin.at[op, c, j],
                        dst_ref=yin.at[op, c, j],
                        send_sem=ya_s.at[op, c, 0],
                        recv_sem=ya_r.at[op, c, j],
                        device_id={"z": j},
                    ).wait_recv()

            given = [yin[op, c, j, end] for end in range(2) for j in range(NBY)]

            def ends(i, carry):
                for end, to in ((0, lax.rem(i + NBY - 1, NBY)), (1, lax.rem(i + 1, NBY))):
                    total = None
                    for k in range(16):
                        term = inverse[k, pl.ds(8 * end + i, 1), :] * given[k]
                        total = term if total is None else total + term
                    yout[op, c, to, 1 - end] = total
                return carry

            lax.fori_loop(0, NBY, ends, 0)
            for i in range(NBY):

                @pl.when(z != i)
                def _():
                    y_answer(op, c, part, i).start()

                @pl.when(z == i)
                def _():
                    yback[op, c, :, pl.ds(pl.multiple_of(part * 8, 8), 8), :] = yout[op, c, i]

    def y_neighbours(op, c):
        for t in range(4):

            @pl.when(z != (4 * c + t) % NBY)
            def _():
                remote(
                    src_ref=yout.at[op, c, 0],
                    dst_ref=yback.at[op, c, :, pl.ds(8 * t, 8), :],
                    send_sem=yb_s.at[op, c, 0],
                    recv_sem=yb_r.at[op, c, t],
                    device_id={"z": (4 * c + t) % NBY},
                ).wait_recv()

        return yback[op, c, 0], yback[op, c, 1]

    def lines(i):
        return pl.ds(i, 1)

    for c in ORDER:
        for k in range(1, 8):
            exchange_in(c, k).wait_recv()
        keep_in(c).wait()
        start_halo(0, c)
        flat = uz.at[c].reshape(38 * BLK, 128)

        def turn(i, carry):
            uy[c, 3 + i] = flat[pl.ds(3 * BLK + i, BLK, stride=BLK), :]
            return carry

        lax.fori_loop(0, BLK, turn, 0)
        start_halo(1, c)

    for c in ORDER:
        wait_halo(1, c)

        def multiply(i, carry):
            prod[i] = uy[c, i] * uy[1, i]
            return carry

        lax.fori_loop(0, 38, multiply, 0)
        solve_lines(derivative_rhs(prod), const_table, gy.at[c])
        start_y_ends(0, c, gy)

    for c in ORDER:
        wait_halo(0, c)
    for c in ORDER:

        def multiply(i, carry):
            prod[i] = uz[c, i] * uz[2, i]
            return carry

        lax.fori_loop(0, 38, multiply, 0)
        solve_lines(derivative_rhs(prod), const_table, gz.at[c])
        start_z_ends(0, c, gz)

    for c in ORDER:
        solve_y_ends(0, c, const_ry)

    for k in range(1, 8):
        exchange_extra(k).wait_recv()
    for c in ORDER:

        def along_x(q, carry):
            rows = pl.ds(pl.multiple_of(3 + 8 * q, 1), 8)
            velocity = uz[c, rows]
            product = (velocity * uz[0, rows]).reshape(256, 128)
            inside = lax.dot_general(
                product,
                dxb[...],
                (((1,), (1,)), ((), ())),
                precision=HIGHEST,
                preferred_element_type=F32,
            ).reshape(8, BLK, 128)
            outside = []
            for low in range(2):
                source = ((q // 2) * 2 + low) * 2 + lax.rem(q, 2)
                outside.append(
                    lax.dot_general(
                        er[source, c],
                        wprof[...],
                        (((0,), (0,)), ((), ())),
                        precision=HIGHEST,
                        preferred_element_type=F32,
                    ).reshape(8, 16, 128)
                )
            total = inside + jnp.concatenate(outside, axis=1)
            w0[c, pl.ds(8 * q, 8)] = velocity - 0.1 * total
            return carry

        lax.fori_loop(0, 4, along_x, 0)

    for c in ORDER:
        before, after = z_neighbours(0, c, const_rz)

        def correct_z(i, carry):
            slope = gz[c, i] - const_table[2, lines(i), :] * before
            slope -= const_table[3, lines(i), :] * after
            w0[c, i] = w0[c, i] - (0.1 * met_z[lines(i), :]) * slope
            return carry

        lax.fori_loop(0, BLK, correct_z, 0)
        flat = w0.at[c].reshape(BLK * BLK, 128)
        before, after = y_neighbours(0, c)

        def correct_y(i, carry):
            slope = gy[c, i] - const_table[2, lines(i), :] * before
            slope -= const_table[3, lines(i), :] * after
            wy[c, 3 + i] = flat[pl.ds(i, BLK, stride=BLK), :] - (0.1 * met_y[lines(i), :]) * slope
            return carry

        lax.fori_loop(0, BLK, correct_y, 0)
        start_halo(2, c)

    for c in ORDER:
        wait_halo(2, c)
        solve_lines(filter_rhs(wy.at[c], slack_y, first_y), tab_y, vy.at[c])
        start_y_ends(1, c, vy)
    for c in ORDER:
        solve_y_ends(1, c, ry)
    for c in ORDER:
        before, after = y_neighbours(1, c)

        def smooth_y(i, carry):
            change = vy[c, i] - tab_y[2, lines(i), :] * before
            change -= tab_y[3, lines(i), :] * after
            vy[c, i] = wy[c, 3 + i] + change
            return carry

        lax.fori_loop(0, BLK, smooth_y, 0)
        flat = vy.at[c].reshape(BLK * BLK, 128)

        def turn(i, carry):
            wz[c, 3 + i] = flat[pl.ds(i, BLK, stride=BLK), :]
            return carry

        lax.fori_loop(0, BLK, turn, 0)
        start_halo(3, c)
    for c in ORDER:
        wait_halo(3, c)
        solve_lines(filter_rhs(wz.at[c], slack_z, first_z), tab_z, vz.at[c])
        start_z_ends(1, c, vz)

    def exchange_out(c, k):
        d = partner(k)
        return remote(
            src_ref=out.at[c, pl.ds(z_rows(d), 8), pl.ds(y_rows(d), 16), :],
            dst_ref=home.at[c, :, :, x_lanes(me)],
            send_sem=tout_s.at[c, k],
            recv_sem=tout_r.at[c, k],
            device_id=d,
        )

    def keep_out(c):
        return pltpu.make_async_copy(
            out.at[c, pl.ds(z_rows(here), 8), pl.ds(y_rows(here), 16), :],
            home.at[c, :, :, x_lanes(me)],
            loc.at[3 + c],
        )

    for c in ORDER:
        before, after = z_neighbours(1, c, rz)

        def smooth_z(i, carry):
            change = vz[c, i] - tab_z[2, lines(i), :] * before
            change -= tab_z[3, lines(i), :] * after
            out[c, i] = wz[c, 3 + i] + change
            return carry

        lax.fori_loop(0, BLK, smooth_z, 0)
        for k in range(1, 8):
            exchange_out(c, k).start()
        keep_out(c).start()

    for k in range(1, 8):
        exchange_extra(k).wait_send()
    for c in ORDER:
        for k in range(1, 8):
            exchange_in(c, k).wait_send()
        for stage in range(4):
            for side in range(2):
                halos[stage](c=c, side=side).wait_send()
        for op in range(2):
            for k in range(1, NBZ):
                z_ends(op, c, k).wait_send()
            for t in range(4):

                @pl.when(z != (4 * c + t) % NBY)
                def _():
                    y_ends(op, c, t).wait_send()

            part = lax.rem(z + NBY - (4 * c) % NBY, NBY)

            @pl.when(part < 4)
            def _():
                for i in range(NBY):

                    @pl.when(z != i)
                    def _():
                        y_answer(op, c, part, i).wait_send()

        for k in range(1, 8):
            exchange_out(c, k).wait()
        keep_out(c).wait()


def on_device(velocity, dx, dy, dz, sx, sy, sz):
    table = tridiagonal_tables(SIDE, BLK)
    vmem = pl.BlockSpec(memory_space=pltpu.VMEM)
    big, wide = (3, BLK, BLK, 128), (3, BLK + 6, BLK, 128)
    scratch = [pltpu.VMEM(s, F32) for s in (
        wide, wide, (BLK + 6, BLK, 128), big, big, big, wide, big, wide, big, big,
        (NBX, 3, 8, 128), (NBX, 3, 8, 128), (128, 128), (NBX, 8, 1024), (NBX, 8, 1024), (64, 1024),
        (8, 128), (256, 128), (256, 128), (4, BLK, 8, 128), (4, BLK, 8, 128), (4, BLK, 128),
        (4, BLK, 128), (BLK, 128), (BLK, 128), (16, 16, 128), (16, 16, 128),
        (2, 3, NBZ, 2, BLK, 128), (2, 3, 2, BLK, 128), (2, 3, NBY, 2, 8, 128),
        (2, 3, NBY, 2, 8, 128), (2, 3, 2, BLK, 128),
    )]
    scratch += [pltpu.SemaphoreType.DMA(s) for s in (
        (17,), (6,), (3, 8), (3, 8), (8,), (8,), (4, 3, 2), (4, 3, 2), (2, 3, NBZ), (2, 3, NBZ),
        (2, 3, 4), (2, 3, NBY), (2, 3, NBY), (2, 3, 4), (3, 8), (3, 8),
    )]
    home = pl.pallas_call(
        kernel,
        out_shape=jax.ShapeDtypeStruct(velocity.shape, F32),
        in_specs=[vmem, pl.BlockSpec(memory_space=pl.ANY)] + [vmem] * 8,
        out_specs=vmem,
        scratch_shapes=scratch,
        compiler_params=pltpu.CompilerParams(
            collective_id=1, has_side_effects=True, vmem_limit_bytes=60 * 1024 * 1024
        ),
        name="blocks",
    )(
        velocity, dx, dy, dz, sy, sz,
        jnp.asarray(lanes(table)),
        jnp.asarray(lanes(reduced_inverse(table, NBY).T)),
        jnp.asarray(lanes(reduced_inverse(table, NBZ).T)),
        jnp.asarray(outside_profile(), F32),
    )
    count_c, slab_z, rows_y, width_x = velocity.shape
    result = lax.dot_general(
        home.reshape(-1, width_x), sx, (((1,), (1,)), ((), ())), precision=HIGHEST
    )
    return result.reshape(velocity.shape)


def solution(mesh):
    fine = Mesh(mesh.devices.reshape(SIZES), AXES)
    spec = P(None, ("x", "yhi", "core"), ("z", "ylo"), None)
    return jax.shard_map(
        on_device,
        mesh=fine,
        in_specs=(spec, P(), P(), P(), P(), P(), P()),
        out_specs=spec,
        check_vma=False,
    )
```

```python
import functools

import jax
import jax.numpy as jnp
import numpy as np
from jax import lax
from jax.experimental import pallas as pl
from jax.experimental.pallas import tpu as pltpu
from jax.sharding import Mesh
from jax.sharding import PartitionSpec as P

AXES = ("z", "ylo", "x", "yhi", "core")
SIZES = (8, 2, 4, 2, 2)
MESH = pl.DeviceIdType.MESH
HIGHEST = lax.Precision.HIGHEST
F32 = jnp.float32
BLK = 32
NBY, NBZ, NBX = 8, 4, 8
ORDER = (1, 2, 0)
SIDE = 9.0 / 20.0
STENCIL = (63.0 / 80.0, 9.0 / 100.0, -7.0 / 1200.0)


def tridiagonal_tables(side, count):
    piv, cp = np.zeros(count), np.zeros(count)
    before = 0.0
    for i in range(count):
        piv[i] = 1.0 / (1.0 - side * before)
        before = cp[i] = side * piv[i]
    first, last = np.zeros(count), np.zeros(count)
    first[0] = cp[0]
    for i in range(1, count):
        first[i] = -cp[i] * first[i - 1]
    last[-1] = cp[-1]
    for i in range(count - 2, -1, -1):
        first[i] -= cp[i] * first[i + 1]
        last[i] = -cp[i] * last[i + 1]
    return np.stack([piv, cp, first, last])


def reduced_inverse(table, blocks):
    first, last = table[2], table[3]
    full = np.eye(16)
    for i in range(blocks):
        before, after = 8 + (i - 1) % blocks, (i + 1) % blocks
        full[i, before] += first[0]
        full[i, after] += last[0]
        full[8 + i, before] += first[-1]
        full[8 + i, after] += last[-1]
    return np.linalg.inv(full)


def pade_off_diagonal(count):
    left = np.eye(count) + SIDE * (np.roll(np.eye(count), 1, 1) + np.roll(np.eye(count), -1, 1))
    right = sum(
        w * (np.roll(np.eye(count), k + 1, 1) - np.roll(np.eye(count), -k - 1, 1))
        for k, w in enumerate(STENCIL)
    )
    return float(np.linalg.solve(left, right)[0, 1])


def outside_profile():
    inner = 122
    matrix = np.eye(inner) + SIDE * (np.eye(inner, k=1) + np.eye(inner, k=-1))
    profile = np.zeros((8, 128))
    for e, row in enumerate((0, 1, 2, 125, 126, 127)):
        profile[e, row] = 1.0
    unit = np.zeros(inner)
    unit[0] = -SIDE
    profile[2, 3:125] = np.linalg.solve(matrix, unit)
    profile[3, 3:125] = np.linalg.solve(matrix, unit[::-1])
    return profile


def iota(shape, dim):
    return lax.broadcasted_iota(jnp.int32, shape, dim)


def wrapped_offset(shape, first_row, count):
    offset = iota(shape, 1) - iota(shape, 0) - first_row
    return jnp.where(offset < 0, offset + count, offset)


def metric_rows(matrix_ref, first_row, count, unit):
    block = matrix_ref[pl.ds(first_row, BLK), :]
    offset = wrapped_offset(block.shape, first_row, count)
    weight = jnp.where(offset == 1, 0.5 / unit, jnp.where(offset == count - 1, -0.5 / unit, 0.0))
    return jnp.broadcast_to(jnp.sum(block * weight, axis=1, keepdims=True), (BLK, 128))


def filter_slack(matrix_ref, count):
    shape = (count, count)
    offset = wrapped_offset(shape, 0, count)
    change = matrix_ref[...] - jnp.where(offset == 0, 1.0, 0.0)
    around = 0.5 * (pltpu.roll(change, 1, 0) + pltpu.roll(change, count - 1, 0))
    sixth = jnp.zeros(shape, F32)
    for k, w in enumerate((-20.0, 15.0, -6.0, 1.0)):
        sixth = jnp.where((offset == k) | (offset == (count - k) % count), w / 64.0, sixth)
    basis = sixth + around
    top = jnp.sum((change + around) * basis, axis=1, keepdims=True)
    return top / jnp.sum(basis * basis, axis=1, keepdims=True)


def block_tables(slack_ref, all_ref):
    def side(i):
        return 0.5 - 0.5 * slack_ref[pl.ds(i, 8, stride=BLK), :]

    def forward(i, carry):
        before, first = carry
        a = side(i)
        piv = 1.0 / (1.0 - a * before)
        cp = a * piv
        first = jnp.where(i == 0, cp, -cp * first)
        all_ref[0, i] = piv
        all_ref[1, i] = cp
        all_ref[2, i] = first
        return cp, first

    zero = jnp.zeros((8, 128), F32)
    lax.fori_loop(0, BLK, forward, (zero, zero))

    def backward(k, carry):
        first, last = carry
        i = BLK - 1 - k
        cp = all_ref[1, i]
        first = all_ref[2, i] - cp * first
        last = jnp.where(k == 0, cp, -cp * last)
        all_ref[2, i] = first
        all_ref[3, i] = last
        return first, last

    lax.fori_loop(0, BLK, backward, (zero, zero))


def invert_reduced(all_ref, blocks):
    sub, lane = iota((8, 128), 0), iota((8, 128), 1)
    before = 8 + jnp.where(sub == 0, blocks - 1, sub - 1)
    after = jnp.where(sub == blocks - 1, 0, sub + 1)
    valid = sub < blocks

    def rows(own, first, last):
        value = jnp.where(lane == own, 1.0, 0.0)
        value += jnp.where(valid & (lane == before), first, 0.0)
        return value + jnp.where(valid & (lane == after), last, 0.0)

    full = jnp.concatenate(
        [
            rows(sub, all_ref[2, 0], all_ref[3, 0]),
            rows(8 + sub, all_ref[2, BLK - 1], all_ref[3, BLK - 1]),
        ],
        axis=0,
    )
    sub, lane = iota((16, 128), 0), iota((16, 128), 1)
    full += jnp.where(lane == 16 + sub, 1.0, 0.0)

    def eliminate(k, full):
        column = jnp.sum(jnp.where(lane == k, full, 0.0), axis=1, keepdims=True)
        row = jnp.sum(jnp.where(sub == k, full, 0.0), axis=0, keepdims=True)
        pivot = jnp.sum(jnp.where(sub == k, column, 0.0), axis=0, keepdims=True)[:, :1]
        row = row / pivot
        return jnp.where(sub == k, row, full - column * row)

    return lax.fori_loop(0, 16, eliminate, full)


def loop(count, body, carry, unroll=8):
    steps = count // unroll

    def several(k, carry):
        for j in range(unroll):
            carry = body(k * unroll + j, carry)
        return carry

    carry = lax.fori_loop(0, steps, several, carry)
    for i in range(steps * unroll, count):
        carry = body(i, carry)
    return carry


def each(count, body, unroll=8):
    def step(i, carry):
        body(i)
        return carry

    loop(count, step, 0, unroll)


def halves(value):
    high = value.astype(jnp.bfloat16)
    return high, (value - high.astype(F32)).astype(jnp.bfloat16)


def contract(a, b, dims):
    return lax.dot_general(a, b, (dims, ((), ())), preferred_element_type=F32)


def solve_lines(rhs, table_ref, out_ref):
    def forward(i, before):
        value = rhs(i) * table_ref[0, pl.ds(i, 1), :] - table_ref[1, pl.ds(i, 1), :] * before
        out_ref[i] = value
        return value

    last = loop(BLK, forward, jnp.zeros((BLK, 128), F32))

    def backward(k, after):
        i = BLK - 2 - k
        value = out_ref[i] - table_ref[1, pl.ds(i, 1), :] * after
        out_ref[i] = value
        return value

    loop(BLK - 1, backward, last)


def derivative_rhs(field):
    def rhs(i):
        total = STENCIL[0] * (field[i + 4] - field[i + 2])
        total += STENCIL[1] * (field[i + 5] - field[i + 1])
        return total + STENCIL[2] * (field[i + 6] - field[i])

    return rhs


def filter_rhs(field, slack_ref, first_row):
    def rhs(i):
        total = (field[i] + field[i + 6]) - 6.0 * (field[i + 1] + field[i + 5])
        total += 15.0 * (field[i + 2] + field[i + 4]) - 20.0 * field[i + 3]
        return total * (slack_ref[pl.ds(first_row + i, 1), :] * (1.0 / 64.0))

    return rhs


def kernel(
    u_hbm,
    dx,
    dy_hbm,
    dz_hbm,
    sy_hbm,
    sz_hbm,
    const_hbm,
    home,
    u,
    dy,
    dz,
    sy,
    sz,
    const,
    uz,
    uy,
    prod,
    gz,
    gy,
    w0,
    wz,
    vz,
    qy,
    vy,
    turned,
    out,
    edge,
    fix,
    es,
    er,
    dxb,
    dtop,
    dbot,
    inner,
    outer,
    slack_y,
    slack_z,
    all_y,
    all_z,
    tab_d,
    tab_y,
    tab_z,
    met_y,
    met_z,
    rdy,
    rdz,
    rsy,
    rsz,
    ze,
    ye,
    dma,
    loc,
    tin_s,
    tin_r,
    es_s,
    es_r,
    halo_s,
    halo_r,
    ze_s,
    ze_r,
    ye_s,
    ye_r,
    tout_s,
    tout_r,
    edge_s,
    edge_r,
):
    z, x = lax.axis_index("z"), lax.axis_index("x")
    ylo, yhi, core = lax.axis_index("ylo"), lax.axis_index("yhi"), lax.axis_index("core")
    me = (yhi * 2 + ylo) * 2 + core
    first_y = pl.multiple_of(z * BLK, BLK)
    first_z = pl.multiple_of(x * BLK, BLK)
    started = []

    def flip(index, bit):
        return 1 - index if bit else index

    def partner(k):
        return {"yhi": flip(yhi, k >> 2), "ylo": flip(ylo, (k >> 1) & 1), "core": flip(core, k & 1)}

    def number(d):
        return (d["yhi"] * 2 + d["ylo"]) * 2 + d["core"]

    def x_lanes(g):
        return pl.ds(pl.multiple_of(g * 128, 128), 128)

    def z_rows(d):
        return pl.multiple_of((d["yhi"] * 2 + d["core"]) * 8, 8)

    def y_rows(d):
        return pl.multiple_of(d["ylo"] * 16, 16)

    def lines(i):
        return pl.ds(i, 1)

    here = {"yhi": yhi, "ylo": ylo, "core": core}
    remote = functools.partial(pltpu.make_async_remote_copy, device_id_type=MESH)

    def start(copy):
        copy.start()
        started.append(copy)

    greeted = [partner(k) for k in range(1, 8)]
    greeted += [{"x": lax.rem(x + k, NBZ)} for k in range(1, NBZ)]
    greeted += [{"z": lax.rem(z + k, NBY)} for k in range(1, NBY)]
    barrier = pltpu.get_barrier_semaphore()
    for d in greeted:
        pl.semaphore_signal(barrier, inc=1, device_id=d, device_id_type=MESH)

    first_x = pl.multiple_of(me * 128, 128)
    loads = [
        pltpu.make_async_copy(dx.at[pl.ds(first_x, 128), pl.ds(first_x, 128)], dxb, dma.at[0])
    ]
    for b in range(NBX):
        loads.append(
            pltpu.make_async_copy(dx.at[pl.ds(b * 128, 8), :], dtop.at[b], dma.at[1 + b])
        )
        loads.append(
            pltpu.make_async_copy(dx.at[pl.ds(b * 128 + 120, 8), :], dbot.at[b], dma.at[9 + b])
        )
    pairs = ((u_hbm, u), (const_hbm, const), (dy_hbm, dy), (dz_hbm, dz), (sy_hbm, sy), (sz_hbm, sz))
    for i, (src, dst) in enumerate(pairs):
        loads.append(pltpu.make_async_copy(src, dst, dma.at[17 + i]))
    for load in loads:
        load.start()

    pl.semaphore_wait(barrier, len(greeted))

    def exchange_in(c, k):
        d = partner(k)
        return remote(
            src_ref=u_hbm.at[c, :, :, x_lanes(number(d))],
            dst_ref=uz.at[c, pl.ds(3 + z_rows(here), 8), pl.ds(y_rows(here), 16), :],
            send_sem=tin_s.at[c, k],
            recv_sem=tin_r.at[c, k],
            device_id=d,
        )

    def keep_in(c):
        return pltpu.make_async_copy(
            u_hbm.at[c, :, :, x_lanes(me)],
            uz.at[c, pl.ds(3 + z_rows(here), 8), pl.ds(y_rows(here), 16), :],
            loc.at[c],
        )

    def begin():
        for c in ORDER:
            for k in range(1, 8):
                start(exchange_in(c, k))
            keep_in(c).start()

    def exchange_extra(k):
        d = partner(k)
        return remote(
            src_ref=es.at[number(d)],
            dst_ref=er.at[me],
            send_sem=es_s.at[k],
            recv_sem=es_r.at[k],
            device_id=d,
        )

    def extras():
        for load in loads:
            load.wait()
        column_block = iota((8, 1024), 1) // 128
        picked = []
        for b in range(NBX):
            rows = jnp.concatenate([dtop[b, 0:3], dbot[b, 5:8], jnp.zeros((2, 1024), F32)], axis=0)
            picked.append(jnp.where(column_block == b, 0.0, rows))
        high, low = halves(jnp.concatenate(picked, axis=0))
        both = jnp.concatenate([high, low], axis=0)
        for c in range(3):
            p_high, p_low = halves((u[c] * u[0]).reshape(128, 1024))
            value = contract(both, p_high, ((1,), (1,)))
            value = value[:64] + value[64:] + contract(high, p_low, ((1,), (1,)))
            es[:, c] = value.reshape(NBX, 8, 128)
        for k in range(1, 8):
            start(exchange_extra(k))
        er[me] = es[me]

    def spread(full, first, out_ref):
        lane = iota(full.shape, 1)

        def one(k):
            column = jnp.sum(jnp.where(lane == first + k, full, 0.0), axis=1, keepdims=True)
            out_ref[k] = jnp.broadcast_to(column, full.shape)

        each(out_ref.shape[0], one, 4)

    def derivative_tables():
        spread(const[0:16, :], 0, rdy)
        spread(const[16:32, :], 0, rdz)
        spread(const[32:64, :], 0, tab_d)
        met_y[...] = metric_rows(dy, first_y, 256, pade_off_diagonal(256)) * 0.1
        met_z[...] = metric_rows(dz, first_z, 128, pade_off_diagonal(128)) * 0.1

    def x_tables():
        unit_x = pade_off_diagonal(1024)
        row, col = iota((128, 128), 0), iota((128, 128), 1)
        ends = jnp.where((row == 0) | (row == 127), 1.0 / unit_x, 0.5 / unit_x)
        weight = jnp.where(col == row + 1, ends, jnp.where(col == row - 1, -ends, 0.0))
        metric = lax.dot_general(
            jnp.ones((8, 128), F32),
            dxb[...] * weight,
            (((1,), (1,)), ((), ())),
            precision=HIGHEST,
            preferred_element_type=F32,
        )
        lane, sub = iota((8, 128), 1), iota((8, 128), 0)

        def metric_at(i):
            return jnp.sum(jnp.where(lane == i, metric, 0.0), axis=1, keepdims=True)

        single = (lane < 3) | (lane > 124)
        at_end = jnp.where(sub == 2, metric_at(2), metric_at(125))
        profile = const[64:72, :] * jnp.where(single, 1.0, metric / at_end)
        high, low = halves(profile)
        outer[...] = jnp.concatenate([high, high, low, jnp.zeros_like(low)], axis=0)
        high, low = halves(dxb[...].T)
        inner[0:128, 0:128] = high
        inner[128:256, 0:128] = high
        inner[0:128, 128:256] = low
        inner[128:256, 128:256] = jnp.zeros_like(low)

    def filter_tables():
        slack_y[...] = jnp.broadcast_to(filter_slack(sy, 256), (256, 128))
        half = jnp.broadcast_to(filter_slack(sz, 128), (128, 128))
        slack_z[0:128, :] = half
        slack_z[128:256, :] = half
        block_tables(slack_y, all_y)
        block_tables(slack_z, all_z)

        def pick(i):
            for t in range(4):
                tab_y[t, lines(i), :] = all_y[t, i, pl.ds(z, 1), :]
                tab_z[t, lines(i), :] = all_z[t, i, pl.ds(x, 1), :]

        each(BLK, pick, 4)
        spread(invert_reduced(all_y, NBY), 16, rsy)
        spread(invert_reduced(all_z, NBZ), 16, rsz)

    def halo(stage, c, side):
        field, axis, size = ((uz, "x", NBZ), (uy, "z", NBY), (wz, "x", NBZ), (qy, "z", NBY))[stage]
        index = {"z": z, "x": x}[axis]
        if side == 0:
            src, dst, to = 32, 0, lax.rem(index + 1, size)
        else:
            src, dst, to = 3, 35, lax.rem(index + size - 1, size)
        return remote(
            src_ref=field.at[c, pl.ds(src, 3)],
            dst_ref=field.at[c, pl.ds(dst, 3)],
            send_sem=halo_s.at[stage, c, side],
            recv_sem=halo_r.at[stage, c, side],
            device_id={axis: to},
        )

    def start_halo(stage, c):
        for side in range(2):
            start(halo(stage, c, side))

    def wait_halo(stage, c):
        for side in range(2):
            halo(stage, c, side).wait_recv()

    def end_copy(axis, op, c, k):
        buf, send, recv = {"x": (ze, ze_s, ze_r), "z": (ye, ye_s, ye_r)}[axis]
        index, size = {"x": (x, NBZ), "z": (z, NBY)}[axis]
        return remote(
            src_ref=buf.at[op, c, index],
            dst_ref=buf.at[op, c, index],
            send_sem=send.at[op, c, k],
            recv_sem=recv.at[op, c, k],
            device_id={axis: lax.rem(index + k, size)},
        )

    def start_ends(axis, op, c, solved):
        buf, index, size = {"x": (ze, x, NBZ), "z": (ye, z, NBY)}[axis]
        buf[op, c, index, 0] = solved[c, 0]
        buf[op, c, index, 1] = solved[c, BLK - 1]
        for k in sorted(range(1, size), key=lambda k: -min(k, size - k)):
            start(end_copy(axis, op, c, k))

    def neighbours(axis, op, c, inverse):
        buf, index, size = {"x": (ze, x, NBZ), "z": (ye, z, NBY)}[axis]
        for k in range(1, size):
            end_copy(axis, op, c, k).wait_recv()
        values = []
        for target in (8 + lax.rem(index + size - 1, size), lax.rem(index + 1, size)):
            total = None
            for j in range(size):
                for end in range(2):
                    term = inverse[8 * end + j, lines(target), :] * buf[op, c, j, end]
                    total = term if total is None else total + term
            values.append(total)
        return values

    def turn(src, dst, first):
        flat = src.reshape(src.shape[0] * BLK, 128)

        def one(i):
            dst[first[1] + i] = flat[pl.ds(first[0] * BLK + i, BLK, stride=BLK), :]

        each(BLK, one)

    def minus_ends(value, table, i, before, after):
        return value - table[2, lines(i), :] * before - table[3, lines(i), :] * after

    def arrive(c):
        for k in range(1, 8):
            exchange_in(c, k).wait_recv()
        keep_in(c).wait()
        start_halo(0, c)
        turn(uz.at[c], uy.at[c], (3, 3))
        start_halo(1, c)

    def slope_y(c):
        wait_halo(1, c)

        def multiply(i):
            prod[i] = uy[c, i] * uy[1, i]

        each(38, multiply)
        solve_lines(derivative_rhs(prod), tab_d, gy.at[c])
        start_ends("z", 0, c, gy)

    def slope_z(c):
        wait_halo(0, c)

        def multiply(i):
            prod[i] = uz[c, i] * uz[2, i]

        each(38, multiply)
        solve_lines(derivative_rhs(prod), tab_d, gz.at[c])
        start_ends("x", 0, c, gz)

    def slope_x(c):
        if c == ORDER[0]:
            for k in range(1, 8):
                exchange_extra(k).wait_recv()

        def part(q, carry):
            rows = pl.ds(3 + 8 * q, 8)
            velocity = uz[c, rows]
            high, low = halves((velocity * uz[0, rows]).reshape(256, 128))
            value = contract(jnp.concatenate([high, low], axis=1), inner[...], ((1,), (0,)))
            total = (value[:, :128] + value[:, 128:]).reshape(8, BLK, 128)
            outside = []
            for low_y in range(2):
                source = ((q // 2) * 2 + low_y) * 2 + lax.rem(q, 2)
                high, low = halves(er[source, c])
                given = jnp.concatenate([high, low, high, jnp.zeros_like(low)], axis=0)
                value = contract(given, outer[...], ((0,), (0,)))
                outside.append(value.reshape(8, 16, 128))
            total += jnp.concatenate(outside, axis=1)
            w0[c, pl.ds(8 * q, 8)] = velocity - 0.1 * total
            return carry

        lax.fori_loop(0, 4, part, 0)

    def advance(c):
        before, after = neighbours("z", 0, c, rdy)

        def correct_y(i):
            gy[c, i] = met_y[lines(i), :] * minus_ends(gy[c, i], tab_d, i, before, after)

        each(BLK, correct_y)
        turn(gy.at[c], turned, (0, 0))
        before_z, after_z = neighbours("x", 0, c, rdz)

        def correct_z(i):
            slope = met_z[lines(i), :] * minus_ends(gz[c, i], tab_d, i, before_z, after_z)
            wz[c, 3 + i] = w0[c, i] - slope - turned[i]

        each(BLK, correct_z)
        start_halo(2, c)

    def smooth_z(c):
        wait_halo(2, c)
        solve_lines(filter_rhs(wz.at[c], slack_z, first_z), tab_z, vz.at[c])
        start_ends("x", 1, c, vz)

    def smoothed_z(c):
        before, after = neighbours("x", 1, c, rsz)

        def one(i):
            turned[i] = wz[c, 3 + i] + minus_ends(vz[c, i], tab_z, i, before, after)

        each(BLK, one)
        turn(turned, qy.at[c], (0, 3))
        start_halo(3, c)

    def exchange_out(c, k):
        d = partner(k)
        return remote(
            src_ref=out.at[c, pl.ds(z_rows(d), 8), pl.ds(y_rows(d), 16), :],
            dst_ref=home.at[c, :, :, x_lanes(me)],
            send_sem=tout_s.at[c, k],
            recv_sem=tout_r.at[c, k],
            device_id=d,
        )

    def keep_out(c):
        return pltpu.make_async_copy(
            out.at[c, pl.ds(z_rows(here), 8), pl.ds(y_rows(here), 16), :],
            home.at[c, :, :, x_lanes(me)],
            loc.at[3 + c],
        )

    def smooth_y(c):
        wait_halo(3, c)
        solve_lines(filter_rhs(qy.at[c], slack_y, first_y), tab_y, vy.at[c])
        start_ends("z", 1, c, vy)

        def one(i):
            turned[i] = qy[c, 3 + i] + vy[c, i]

        each(BLK, one)
        turn(turned, out.at[c], (0, 0))
        for k in (4, 5, 2, 6, 3, 7, 1):
            start(exchange_out(c, k))
        keep_out(c).start()

    def edge_copy(c, k):
        d = partner(k)
        return remote(
            src_ref=edge.at[c, :, pl.ds(z_rows(d), 8), :],
            dst_ref=fix.at[c, :, :, x_lanes(me)],
            send_sem=edge_s.at[c, k],
            recv_sem=edge_r.at[c, k],
            device_id=d,
        )

    def correct(c):
        before, after = neighbours("z", 1, c, rsy)
        edge[c, 0] = before
        edge[c, 1] = after
        for k in (4, 5, 2, 6, 3, 7, 1):
            start(edge_copy(c, k))
        fix[c, :, :, x_lanes(me)] = edge[c, :, pl.ds(z_rows(here), 8), :]

    def leave(c):
        for k in range(1, 8):
            exchange_out(c, k).wait_recv()
        keep_out(c).wait()
        for k in range(1, 8):
            edge_copy(c, k).wait_recv()
        first = tab_y[2, pl.ds(y_rows(here), 16), :]
        last = tab_y[3, pl.ds(y_rows(here), 16), :]

        def one(g):
            lanes = x_lanes(g)
            before, after = fix[c, 0, :, lanes], fix[c, 1, :, lanes]
            for i in range(8):
                value = home[c, i, :, lanes] - first * before[i : i + 1]
                home[c, i, :, lanes] = value - last * after[i : i + 1]

        each(8, one, 2)

    one, two, three = ORDER
    steps = [
        (begin,),
        (extras,),
        (derivative_tables,),
        (arrive, one),
        (x_tables,),
        (slope_y, one),
        (filter_tables,),
        (arrive, two),
        (slope_y, two),
        (slope_z, two),
        (slope_z, one),
        (arrive, three),
        (slope_x, one),
        (advance, one),
        (slope_y, three),
        (slope_z, three),
        (slope_x, two),
        (advance, two),
        (smooth_z, one),
        (slope_x, three),
        (smooth_z, two),
        (advance, three),
        (smoothed_z, one),
        (smoothed_z, two),
        (smooth_z, three),
        (smooth_y, one),
        (smooth_y, two),
        (smoothed_z, three),
        (correct, one),
        (correct, two),
        (smooth_y, three),
        (leave, one),
        (leave, two),
        (correct, three),
        (leave, three),
    ]
    for step in steps[:STOP]:
        step[0](*step[1:])
    for copy in started:
        copy.wait_send()


STOP = 99


def on_device(velocity, dx, dy, dz, sx, sy, sz):
    table = tridiagonal_tables(SIDE, BLK)
    const = np.zeros((72, 128), np.float32)
    const[0:16, :16] = reduced_inverse(table, NBY)
    const[16:32, :16] = reduced_inverse(table, NBZ)
    const[32:64, :4] = table.T
    const[64:72] = outside_profile()
    vmem = pl.BlockSpec(memory_space=pltpu.VMEM)
    big, wide, one = (3, BLK, BLK, 128), (3, BLK + 6, BLK, 128), (BLK, BLK, 128)
    shapes = (
        velocity.shape, (256, 256), (128, 128), (256, 256), (128, 128), (72, 128),
        wide, wide, (BLK + 6, BLK, 128), big, big, big, wide, big, wide, big, one, big,
        (3, 2, BLK, 128), (3, 2, 8, 1024),
        (NBX, 3, 8, 128), (NBX, 3, 8, 128), (128, 128), (NBX, 8, 1024), (NBX, 8, 1024),
    )
    scratch = [pltpu.VMEM(s, F32) for s in shapes]
    scratch += [pltpu.VMEM((256, 256), jnp.bfloat16), pltpu.VMEM((32, 128), jnp.bfloat16)]
    shapes = (
        (256, 128), (256, 128), (4, BLK, 8, 128), (4, BLK, 8, 128),
        (4, BLK, 128), (4, BLK, 128), (4, BLK, 128), (BLK, 128), (BLK, 128),
        (16, 16, 128), (16, 16, 128), (16, 16, 128), (16, 16, 128),
        (2, 3, NBZ, 2, BLK, 128), (2, 3, NBY, 2, BLK, 128),
    )
    scratch += [pltpu.VMEM(s, F32) for s in shapes]
    counts = (
        (23,), (6,), (3, 8), (3, 8), (8,), (8,), (4, 3, 2), (4, 3, 2),
        (2, 3, NBZ), (2, 3, NBZ), (2, 3, NBY), (2, 3, NBY), (3, 8), (3, 8),
        (3, 8), (3, 8),
    )
    scratch += [pltpu.SemaphoreType.DMA(s) for s in counts]
    home = pl.pallas_call(
        kernel,
        out_shape=jax.ShapeDtypeStruct(velocity.shape, F32),
        in_specs=[pl.BlockSpec(memory_space=pl.ANY)] * 7,
        out_specs=vmem,
        scratch_shapes=scratch,
        compiler_params=pltpu.CompilerParams(
            collective_id=1, has_side_effects=True, vmem_limit_bytes=60 * 1024 * 1024
        ),
        name="blocks",
    )(velocity, dx, dy, dz, sy, sz, jnp.asarray(const))
    width_x = velocity.shape[3]
    result = lax.dot_general(
        home.reshape(-1, width_x), sx, (((1,), (1,)), ((), ())), precision=lax.Precision.HIGH
    )
    return result.reshape(velocity.shape)


def solution(mesh):
    fine = Mesh(mesh.devices.reshape(SIZES), AXES)
    spec = P(None, ("x", "yhi", "core"), ("z", "ylo"), None)
    return jax.shard_map(
        on_device,
        mesh=fine,
        in_specs=(spec, P(), P(), P(), P(), P(), P()),
        out_specs=spec,
        check_vma=False,
    )
```

```python
import functools

import jax
import jax.numpy as jnp
import numpy as np
from jax import lax
from jax.experimental import pallas as pl
from jax.experimental.pallas import tpu as pltpu
from jax.sharding import Mesh
from jax.sharding import PartitionSpec as P

AXES = ("z", "ylo", "x", "yhi", "core")
SIZES = (8, 2, 4, 2, 2)
MESH = pl.DeviceIdType.MESH
HIGHEST = lax.Precision.HIGHEST
F32 = jnp.float32
BLK = 32
NBY, NBZ, NBX = 8, 4, 8
ORDER = (1, 2, 0)
SIDE = 9.0 / 20.0
STENCIL = (63.0 / 80.0, 9.0 / 100.0, -7.0 / 1200.0)


def tridiagonal_tables(side, count):
    piv, cp = np.zeros(count), np.zeros(count)
    before = 0.0
    for i in range(count):
        piv[i] = 1.0 / (1.0 - side * before)
        before = cp[i] = side * piv[i]
    first, last = np.zeros(count), np.zeros(count)
    first[0] = cp[0]
    for i in range(1, count):
        first[i] = -cp[i] * first[i - 1]
    last[-1] = cp[-1]
    for i in range(count - 2, -1, -1):
        first[i] -= cp[i] * first[i + 1]
        last[i] = -cp[i] * last[i + 1]
    return np.stack([piv, cp, first, last])


def reduced_inverse(table, blocks):
    first, last = table[2], table[3]
    full = np.eye(16)
    for i in range(blocks):
        before, after = 8 + (i - 1) % blocks, (i + 1) % blocks
        full[i, before] += first[0]
        full[i, after] += last[0]
        full[8 + i, before] += first[-1]
        full[8 + i, after] += last[-1]
    return np.linalg.inv(full)


def pade_off_diagonal(count):
    left = np.eye(count) + SIDE * (np.roll(np.eye(count), 1, 1) + np.roll(np.eye(count), -1, 1))
    right = sum(
        w * (np.roll(np.eye(count), k + 1, 1) - np.roll(np.eye(count), -k - 1, 1))
        for k, w in enumerate(STENCIL)
    )
    return float(np.linalg.solve(left, right)[0, 1])


def outside_profile():
    inner = 122
    matrix = np.eye(inner) + SIDE * (np.eye(inner, k=1) + np.eye(inner, k=-1))
    profile = np.zeros((8, 128))
    for e, row in enumerate((0, 1, 2, 125, 126, 127)):
        profile[e, row] = 1.0
    unit = np.zeros(inner)
    unit[0] = -SIDE
    profile[2, 3:125] = np.linalg.solve(matrix, unit)
    profile[3, 3:125] = np.linalg.solve(matrix, unit[::-1])
    return profile


def iota(shape, dim):
    return lax.broadcasted_iota(jnp.int32, shape, dim)


def wrapped_offset(shape, first_row, count):
    offset = iota(shape, 1) - iota(shape, 0) - first_row
    return jnp.where(offset < 0, offset + count, offset)


def metric_rows(matrix_ref, first_row, count, unit):
    block = matrix_ref[pl.ds(first_row, BLK), :]
    offset = wrapped_offset(block.shape, first_row, count)
    weight = jnp.where(offset == 1, 0.5 / unit, jnp.where(offset == count - 1, -0.5 / unit, 0.0))
    return jnp.broadcast_to(jnp.sum(block * weight, axis=1, keepdims=True), (BLK, 128))


def filter_slack(matrix_ref, count):
    shape = (count, count)
    offset = wrapped_offset(shape, 0, count)
    change = matrix_ref[...] - jnp.where(offset == 0, 1.0, 0.0)
    around = 0.5 * (pltpu.roll(change, 1, 0) + pltpu.roll(change, count - 1, 0))
    sixth = jnp.zeros(shape, F32)
    for k, w in enumerate((-20.0, 15.0, -6.0, 1.0)):
        sixth = jnp.where((offset == k) | (offset == (count - k) % count), w / 64.0, sixth)
    basis = sixth + around
    top = jnp.sum((change + around) * basis, axis=1, keepdims=True)
    return top / jnp.sum(basis * basis, axis=1, keepdims=True)


def block_tables(slack_ref, all_ref):
    def side(i):
        return 0.5 - 0.5 * slack_ref[pl.ds(i, 8, stride=BLK), :]

    def forward(i, carry):
        before, first = carry
        a = side(i)
        piv = 1.0 / (1.0 - a * before)
        cp = a * piv
        first = jnp.where(i == 0, cp, -cp * first)
        all_ref[0, i] = piv
        all_ref[1, i] = cp
        all_ref[2, i] = first
        return cp, first

    zero = jnp.zeros((8, 128), F32)
    lax.fori_loop(0, BLK, forward, (zero, zero))

    def backward(k, carry):
        first, last = carry
        i = BLK - 1 - k
        cp = all_ref[1, i]
        first = all_ref[2, i] - cp * first
        last = jnp.where(k == 0, cp, -cp * last)
        all_ref[2, i] = first
        all_ref[3, i] = last
        return first, last

    lax.fori_loop(0, BLK, backward, (zero, zero))


def invert_reduced(all_ref, blocks):
    sub, lane = iota((8, 128), 0), iota((8, 128), 1)
    before = 8 + jnp.where(sub == 0, blocks - 1, sub - 1)
    after = jnp.where(sub == blocks - 1, 0, sub + 1)
    valid = sub < blocks

    def rows(own, first, last):
        value = jnp.where(lane == own, 1.0, 0.0)
        value += jnp.where(valid & (lane == before), first, 0.0)
        return value + jnp.where(valid & (lane == after), last, 0.0)

    full = jnp.concatenate(
        [
            rows(sub, all_ref[2, 0], all_ref[3, 0]),
            rows(8 + sub, all_ref[2, BLK - 1], all_ref[3, BLK - 1]),
        ],
        axis=0,
    )
    sub, lane = iota((16, 128), 0), iota((16, 128), 1)
    full += jnp.where(lane == 16 + sub, 1.0, 0.0)

    def eliminate(k, full):
        column = jnp.sum(jnp.where(lane == k, full, 0.0), axis=1, keepdims=True)
        row = jnp.sum(jnp.where(sub == k, full, 0.0), axis=0, keepdims=True)
        pivot = jnp.sum(jnp.where(sub == k, column, 0.0), axis=0, keepdims=True)[:, :1]
        row = row / pivot
        return jnp.where(sub == k, row, full - column * row)

    return lax.fori_loop(0, 16, eliminate, full)


def loop(count, body, carry, unroll=8):
    steps = count // unroll

    def several(k, carry):
        for j in range(unroll):
            carry = body(k * unroll + j, carry)
        return carry

    carry = lax.fori_loop(0, steps, several, carry)
    for i in range(steps * unroll, count):
        carry = body(i, carry)
    return carry


def each(count, body, unroll=8):
    def step(i, carry):
        body(i)
        return carry

    loop(count, step, 0, unroll)


def halves(value):
    high = value.astype(jnp.bfloat16)
    return high, (value - high.astype(F32)).astype(jnp.bfloat16)


def contract(a, b, dims):
    return lax.dot_general(a, b, (dims, ((), ())), preferred_element_type=F32)


def solve_lines(rhs, table_ref, out_ref):
    def forward(i, before):
        value = rhs(i) * table_ref[0, pl.ds(i, 1), :] - table_ref[1, pl.ds(i, 1), :] * before
        out_ref[i] = value
        return value

    last = loop(BLK, forward, jnp.zeros((BLK, 128), F32))

    def backward(k, after):
        i = BLK - 2 - k
        value = out_ref[i] - table_ref[1, pl.ds(i, 1), :] * after
        out_ref[i] = value
        return value

    loop(BLK - 1, backward, last)


def derivative_rhs(field):
    def rhs(i):
        total = STENCIL[0] * (field[i + 4] - field[i + 2])
        total += STENCIL[1] * (field[i + 5] - field[i + 1])
        return total + STENCIL[2] * (field[i + 6] - field[i])

    return rhs


def filter_rhs(field, slack_ref, first_row):
    def rhs(i):
        total = (field[i] + field[i + 6]) - 6.0 * (field[i + 1] + field[i + 5])
        total += 15.0 * (field[i + 2] + field[i + 4]) - 20.0 * field[i + 3]
        return total * (slack_ref[pl.ds(first_row + i, 1), :] * (1.0 / 64.0))

    return rhs


def kernel(
    u_hbm,
    dx,
    dy_hbm,
    dz_hbm,
    sy_hbm,
    sz_hbm,
    const_hbm,
    home,
    u,
    dy,
    dz,
    sy,
    sz,
    const,
    uz,
    uy,
    prod,
    gz,
    gy,
    w0,
    wz,
    vz,
    qy,
    vy,
    turned,
    out,
    edge,
    fix,
    es,
    er,
    dxb,
    dtop,
    dbot,
    inner,
    outer,
    slack_y,
    slack_z,
    all_y,
    all_z,
    tab_d,
    tab_y,
    tab_z,
    met_y,
    met_z,
    rdy,
    rdz,
    rsy,
    rsz,
    ze,
    ye,
    dma,
    loc,
    tin_s,
    tin_r,
    es_s,
    es_r,
    halo_s,
    halo_r,
    ze_s,
    ze_r,
    ye_s,
    ye_r,
    tout_s,
    tout_r,
    edge_s,
    edge_r,
):
    z, x = lax.axis_index("z"), lax.axis_index("x")
    ylo, yhi, core = lax.axis_index("ylo"), lax.axis_index("yhi"), lax.axis_index("core")
    me = (yhi * 2 + ylo) * 2 + core
    first_y = pl.multiple_of(z * BLK, BLK)
    first_z = pl.multiple_of(x * BLK, BLK)
    started = []

    def flip(index, bit):
        return 1 - index if bit else index

    def partner(k):
        return {"yhi": flip(yhi, k >> 2), "ylo": flip(ylo, (k >> 1) & 1), "core": flip(core, k & 1)}

    def number(d):
        return (d["yhi"] * 2 + d["ylo"]) * 2 + d["core"]

    def x_lanes(g):
        return pl.ds(pl.multiple_of(g * 128, 128), 128)

    def z_rows(d):
        return pl.multiple_of((d["yhi"] * 2 + d["core"]) * 8, 8)

    def y_rows(d):
        return pl.multiple_of(d["ylo"] * 16, 16)

    def lines(i):
        return pl.ds(i, 1)

    here = {"yhi": yhi, "ylo": ylo, "core": core}
    remote = functools.partial(pltpu.make_async_remote_copy, device_id_type=MESH)

    def start(copy):
        copy.start()
        started.append(copy)

    greeted = [partner(k) for k in range(1, 8)]
    greeted += [{"x": lax.rem(x + k, NBZ)} for k in range(1, NBZ)]
    greeted += [{"z": lax.rem(z + k, NBY)} for k in range(1, NBY)]
    barrier = pltpu.get_barrier_semaphore()
    for d in greeted:
        pl.semaphore_signal(barrier, inc=1, device_id=d, device_id_type=MESH)

    first_x = pl.multiple_of(me * 128, 128)
    loads = [
        pltpu.make_async_copy(dx.at[pl.ds(first_x, 128), pl.ds(first_x, 128)], dxb, dma.at[0])
    ]
    for b in range(NBX):
        loads.append(
            pltpu.make_async_copy(dx.at[pl.ds(b * 128, 8), :], dtop.at[b], dma.at[1 + b])
        )
        loads.append(
            pltpu.make_async_copy(dx.at[pl.ds(b * 128 + 120, 8), :], dbot.at[b], dma.at[9 + b])
        )
    pairs = ((u_hbm, u), (const_hbm, const), (dy_hbm, dy), (dz_hbm, dz), (sy_hbm, sy), (sz_hbm, sz))
    for i, (src, dst) in enumerate(pairs):
        loads.append(pltpu.make_async_copy(src, dst, dma.at[17 + i]))
    for load in loads:
        load.start()

    pl.semaphore_wait(barrier, len(greeted))

    def exchange_in(c, k):
        d = partner(k)
        return remote(
            src_ref=u_hbm.at[c, :, :, x_lanes(number(d))],
            dst_ref=uz.at[c, pl.ds(3 + z_rows(here), 8), pl.ds(y_rows(here), 16), :],
            send_sem=tin_s.at[c, k],
            recv_sem=tin_r.at[c, k],
            device_id=d,
        )

    def keep_in(c):
        return pltpu.make_async_copy(
            u_hbm.at[c, :, :, x_lanes(me)],
            uz.at[c, pl.ds(3 + z_rows(here), 8), pl.ds(y_rows(here), 16), :],
            loc.at[c],
        )

    far_first = (4, 5, 2, 6, 3, 7, 1)

    def begin():
        for c in ORDER[:2]:
            for k in far_first:
                exchange_in(c, k).start()
            keep_in(c).start()

    def begin_last():
        keep_in(ORDER[2]).start()
        for k in far_first:
            for c in ORDER[:2]:
                exchange_in(c, k).wait_send()
            start(exchange_in(ORDER[2], k))

    def exchange_extra(k):
        d = partner(k)
        return remote(
            src_ref=es.at[number(d)],
            dst_ref=er.at[me],
            send_sem=es_s.at[k],
            recv_sem=es_r.at[k],
            device_id=d,
        )

    def extras():
        for load in loads:
            load.wait()
        column_block = iota((8, 1024), 1) // 128
        picked = []
        for b in range(NBX):
            rows = jnp.concatenate([dtop[b, 0:3], dbot[b, 5:8], jnp.zeros((2, 1024), F32)], axis=0)
            picked.append(jnp.where(column_block == b, 0.0, rows))
        high, low = halves(jnp.concatenate(picked, axis=0))
        both = jnp.concatenate([high, low], axis=0)
        for c in range(3):
            p_high, p_low = halves((u[c] * u[0]).reshape(128, 1024))
            value = contract(both, p_high, ((1,), (1,)))
            value = value[:64] + value[64:] + contract(high, p_low, ((1,), (1,)))
            es[:, c] = value.reshape(NBX, 8, 128)
        for k in range(1, 8):
            start(exchange_extra(k))
        er[me] = es[me]

    def spread(full, first, out_ref):
        lane = iota(full.shape, 1)

        def one(k):
            column = jnp.sum(jnp.where(lane == first + k, full, 0.0), axis=1, keepdims=True)
            out_ref[k] = jnp.broadcast_to(column, full.shape)

        each(out_ref.shape[0], one, 4)

    def derivative_tables():
        spread(const[0:16, :], 0, rdy)
        spread(const[16:32, :], 0, rdz)
        spread(const[32:64, :], 0, tab_d)
        met_y[...] = metric_rows(dy, first_y, 256, pade_off_diagonal(256)) * 0.1
        met_z[...] = metric_rows(dz, first_z, 128, pade_off_diagonal(128)) * 0.1

    def x_tables():
        unit_x = pade_off_diagonal(1024)
        row, col = iota((128, 128), 0), iota((128, 128), 1)
        ends = jnp.where((row == 0) | (row == 127), 1.0 / unit_x, 0.5 / unit_x)
        weight = jnp.where(col == row + 1, ends, jnp.where(col == row - 1, -ends, 0.0))
        metric = lax.dot_general(
            jnp.ones((8, 128), F32),
            dxb[...] * weight,
            (((1,), (1,)), ((), ())),
            precision=HIGHEST,
            preferred_element_type=F32,
        )
        lane, sub = iota((8, 128), 1), iota((8, 128), 0)

        def metric_at(i):
            return jnp.sum(jnp.where(lane == i, metric, 0.0), axis=1, keepdims=True)

        single = (lane < 3) | (lane > 124)
        at_end = jnp.where(sub == 2, metric_at(2), metric_at(125))
        profile = const[64:72, :] * jnp.where(single, 1.0, metric / at_end)
        high, low = halves(profile)
        outer[...] = jnp.concatenate([high, high, low, jnp.zeros_like(low)], axis=0)
        high, low = halves(dxb[...].T)
        inner[0:128, 0:128] = high
        inner[128:256, 0:128] = high
        inner[0:128, 128:256] = low
        inner[128:256, 128:256] = jnp.zeros_like(low)

    def filter_tables():
        slack_y[...] = jnp.broadcast_to(filter_slack(sy, 256), (256, 128))
        half = jnp.broadcast_to(filter_slack(sz, 128), (128, 128))
        slack_z[0:128, :] = half
        slack_z[128:256, :] = half
        block_tables(slack_y, all_y)
        block_tables(slack_z, all_z)

        def pick(i):
            for t in range(4):
                tab_y[t, lines(i), :] = all_y[t, i, pl.ds(z, 1), :]
                tab_z[t, lines(i), :] = all_z[t, i, pl.ds(x, 1), :]

        each(BLK, pick, 4)
        spread(invert_reduced(all_y, NBY), 16, rsy)
        spread(invert_reduced(all_z, NBZ), 16, rsz)

    def halo(stage, c, side):
        field, axis, size = ((uz, "x", NBZ), (uy, "z", NBY), (wz, "x", NBZ), (qy, "z", NBY))[stage]
        index = {"z": z, "x": x}[axis]
        if side == 0:
            src, dst, to = 32, 0, lax.rem(index + 1, size)
        else:
            src, dst, to = 3, 35, lax.rem(index + size - 1, size)
        return remote(
            src_ref=field.at[c, pl.ds(src, 3)],
            dst_ref=field.at[c, pl.ds(dst, 3)],
            send_sem=halo_s.at[stage, c, side],
            recv_sem=halo_r.at[stage, c, side],
            device_id={axis: to},
        )

    def start_halo(stage, c):
        for side in range(2):
            start(halo(stage, c, side))

    def wait_halo(stage, c):
        for side in range(2):
            halo(stage, c, side).wait_recv()

    def end_copy(axis, op, c, k):
        buf, send, recv = {"x": (ze, ze_s, ze_r), "z": (ye, ye_s, ye_r)}[axis]
        index, size = {"x": (x, NBZ), "z": (z, NBY)}[axis]
        return remote(
            src_ref=buf.at[op, c, index],
            dst_ref=buf.at[op, c, index],
            send_sem=send.at[op, c, k],
            recv_sem=recv.at[op, c, k],
            device_id={axis: lax.rem(index + k, size)},
        )

    def start_ends(axis, op, c, solved):
        buf, index, size = {"x": (ze, x, NBZ), "z": (ye, z, NBY)}[axis]
        buf[op, c, index, 0] = solved[c, 0]
        buf[op, c, index, 1] = solved[c, BLK - 1]
        for k in sorted(range(1, size), key=lambda k: -min(k, size - k)):
            start(end_copy(axis, op, c, k))

    def neighbours(axis, op, c, inverse):
        buf, index, size = {"x": (ze, x, NBZ), "z": (ye, z, NBY)}[axis]
        for k in range(1, size):
            end_copy(axis, op, c, k).wait_recv()
        values = []
        for target in (8 + lax.rem(index + size - 1, size), lax.rem(index + 1, size)):
            total = None
            for j in range(size):
                for end in range(2):
                    term = inverse[8 * end + j, lines(target), :] * buf[op, c, j, end]
                    total = term if total is None else total + term
            values.append(total)
        return values

    def turn(src, dst, first):
        flat = src.reshape(src.shape[0] * BLK, 128)

        def one(i):
            dst[first[1] + i] = flat[pl.ds(first[0] * BLK + i, BLK, stride=BLK), :]

        each(BLK, one)

    def minus_ends(value, table, i, before, after):
        return value - table[2, lines(i), :] * before - table[3, lines(i), :] * after

    def arrive(c):
        for k in range(1, 8):
            exchange_in(c, k).wait_recv()
        keep_in(c).wait()
        start_halo(0, c)
        turn(uz.at[c], uy.at[c], (3, 3))
        start_halo(1, c)

    def slope_y(c):
        wait_halo(1, c)

        def multiply(i):
            prod[i] = uy[c, i] * uy[1, i]

        each(38, multiply)
        solve_lines(derivative_rhs(prod), tab_d, gy.at[c])
        start_ends("z", 0, c, gy)

    def slope_z(c):
        wait_halo(0, c)

        def multiply(i):
            prod[i] = uz[c, i] * uz[2, i]

        each(38, multiply)
        solve_lines(derivative_rhs(prod), tab_d, gz.at[c])
        start_ends("x", 0, c, gz)

    def slope_x(c):
        if c == ORDER[0]:
            for k in range(1, 8):
                exchange_extra(k).wait_recv()

        def part(q, carry):
            rows = pl.ds(3 + 8 * q, 8)
            velocity = uz[c, rows]
            high, low = halves((velocity * uz[0, rows]).reshape(256, 128))
            value = contract(jnp.concatenate([high, low], axis=1), inner[...], ((1,), (0,)))
            total = (value[:, :128] + value[:, 128:]).reshape(8, BLK, 128)
            outside = []
            for low_y in range(2):
                source = ((q // 2) * 2 + low_y) * 2 + lax.rem(q, 2)
                high, low = halves(er[source, c])
                given = jnp.concatenate([high, low, high, jnp.zeros_like(low)], axis=0)
                value = contract(given, outer[...], ((0,), (0,)))
                outside.append(value.reshape(8, 16, 128))
            total += jnp.concatenate(outside, axis=1)
            w0[c, pl.ds(8 * q, 8)] = velocity - 0.1 * total
            return carry

        lax.fori_loop(0, 4, part, 0)

    def advance(c):
        before, after = neighbours("z", 0, c, rdy)

        def correct_y(i):
            gy[c, i] = met_y[lines(i), :] * minus_ends(gy[c, i], tab_d, i, before, after)

        each(BLK, correct_y)
        turn(gy.at[c], turned, (0, 0))
        before_z, after_z = neighbours("x", 0, c, rdz)

        def correct_z(i):
            slope = met_z[lines(i), :] * minus_ends(gz[c, i], tab_d, i, before_z, after_z)
            wz[c, 3 + i] = w0[c, i] - slope - turned[i]

        each(BLK, correct_z)
        start_halo(2, c)

    def smooth_z(c):
        wait_halo(2, c)
        solve_lines(filter_rhs(wz.at[c], slack_z, first_z), tab_z, vz.at[c])
        start_ends("x", 1, c, vz)

    def smoothed_z(c):
        before, after = neighbours("x", 1, c, rsz)

        def one(i):
            turned[i] = wz[c, 3 + i] + minus_ends(vz[c, i], tab_z, i, before, after)

        each(BLK, one)
        turn(turned, qy.at[c], (0, 3))
        start_halo(3, c)

    def exchange_out(c, k):
        d = partner(k)
        return remote(
            src_ref=out.at[c, pl.ds(z_rows(d), 8), pl.ds(y_rows(d), 16), :],
            dst_ref=home.at[c, :, :, x_lanes(me)],
            send_sem=tout_s.at[c, k],
            recv_sem=tout_r.at[c, k],
            device_id=d,
        )

    def keep_out(c):
        return pltpu.make_async_copy(
            out.at[c, pl.ds(z_rows(here), 8), pl.ds(y_rows(here), 16), :],
            home.at[c, :, :, x_lanes(me)],
            loc.at[3 + c],
        )

    def smooth_y(c):
        wait_halo(3, c)
        solve_lines(filter_rhs(qy.at[c], slack_y, first_y), tab_y, vy.at[c])
        start_ends("z", 1, c, vy)

        def one(i):
            turned[i] = qy[c, 3 + i] + vy[c, i]

        each(BLK, one)
        turn(turned, out.at[c], (0, 0))
        for k in far_first:
            start(exchange_out(c, k))
        keep_out(c).start()

    def edge_copy(c, k):
        d = partner(k)
        return remote(
            src_ref=edge.at[c, :, pl.ds(z_rows(d), 8), :],
            dst_ref=fix.at[c, :, :, x_lanes(me)],
            send_sem=edge_s.at[c, k],
            recv_sem=edge_r.at[c, k],
            device_id=d,
        )

    def correct(c):
        before, after = neighbours("z", 1, c, rsy)
        edge[c, 0] = before
        edge[c, 1] = after
        for k in far_first:
            start(edge_copy(c, k))
        fix[c, :, :, x_lanes(me)] = edge[c, :, pl.ds(z_rows(here), 8), :]

    def leave(c):
        for k in range(1, 8):
            exchange_out(c, k).wait_recv()
        keep_out(c).wait()
        for k in range(1, 8):
            edge_copy(c, k).wait_recv()
        first = tab_y[2, pl.ds(y_rows(here), 16), :]
        last = tab_y[3, pl.ds(y_rows(here), 16), :]

        def one(g):
            lanes = x_lanes(g)
            before, after = fix[c, 0, :, lanes], fix[c, 1, :, lanes]
            for i in range(8):
                value = home[c, i, :, lanes] - first * before[i : i + 1]
                home[c, i, :, lanes] = value - last * after[i : i + 1]

        each(8, one, 2)

    one, two, three = ORDER
    steps = [
        (begin,),
        (extras,),
        (derivative_tables,),
        (x_tables,),
        (filter_tables,),
        (begin_last,),
        (arrive, one),
        (arrive, two),
        (slope_y, one),
        (slope_y, two),
        (slope_z, two),
        (slope_z, one),
        (arrive, three),
        (slope_x, one),
        (advance, one),
        (slope_y, three),
        (slope_z, three),
        (slope_x, two),
        (advance, two),
        (smooth_z, one),
        (slope_x, three),
        (smooth_z, two),
        (smoothed_z, one),
        (advance, three),
        (smoothed_z, two),
        (smooth_y, one),
        (smooth_z, three),
        (smooth_y, two),
        (smoothed_z, three),
        (correct, one),
        (smooth_y, three),
        (correct, two),
        (leave, one),
        (correct, three),
        (leave, two),
        (leave, three),
    ]
    for step in steps[:STOP]:
        step[0](*step[1:])
    for copy in started:
        copy.wait_send()


STOP = 99


def on_device(velocity, dx, dy, dz, sx, sy, sz):
    table = tridiagonal_tables(SIDE, BLK)
    const = np.zeros((72, 128), np.float32)
    const[0:16, :16] = reduced_inverse(table, NBY)
    const[16:32, :16] = reduced_inverse(table, NBZ)
    const[32:64, :4] = table.T
    const[64:72] = outside_profile()
    vmem = pl.BlockSpec(memory_space=pltpu.VMEM)
    big, wide, one = (3, BLK, BLK, 128), (3, BLK + 6, BLK, 128), (BLK, BLK, 128)
    shapes = (
        velocity.shape, (256, 256), (128, 128), (256, 256), (128, 128), (72, 128),
        wide, wide, (BLK + 6, BLK, 128), big, big, big, wide, big, wide, big, one, big,
        (3, 2, BLK, 128), (3, 2, 8, 1024),
        (NBX, 3, 8, 128), (NBX, 3, 8, 128), (128, 128), (NBX, 8, 1024), (NBX, 8, 1024),
    )
    scratch = [pltpu.VMEM(s, F32) for s in shapes]
    scratch += [pltpu.VMEM((256, 256), jnp.bfloat16), pltpu.VMEM((32, 128), jnp.bfloat16)]
    shapes = (
        (256, 128), (256, 128), (4, BLK, 8, 128), (4, BLK, 8, 128),
        (4, BLK, 128), (4, BLK, 128), (4, BLK, 128), (BLK, 128), (BLK, 128),
        (16, 16, 128), (16, 16, 128), (16, 16, 128), (16, 16, 128),
        (2, 3, NBZ, 2, BLK, 128), (2, 3, NBY, 2, BLK, 128),
    )
    scratch += [pltpu.VMEM(s, F32) for s in shapes]
    counts = (
        (23,), (6,), (3, 8), (3, 8), (8,), (8,), (4, 3, 2), (4, 3, 2),
        (2, 3, NBZ), (2, 3, NBZ), (2, 3, NBY), (2, 3, NBY), (3, 8), (3, 8),
        (3, 8), (3, 8),
    )
    scratch += [pltpu.SemaphoreType.DMA(s) for s in counts]
    home = pl.pallas_call(
        kernel,
        out_shape=jax.ShapeDtypeStruct(velocity.shape, F32),
        in_specs=[pl.BlockSpec(memory_space=pl.ANY)] * 7,
        out_specs=vmem,
        scratch_shapes=scratch,
        compiler_params=pltpu.CompilerParams(
            collective_id=1, has_side_effects=True, vmem_limit_bytes=60 * 1024 * 1024
        ),
        name="blocks",
    )(velocity, dx, dy, dz, sy, sz, jnp.asarray(const))
    width_x = velocity.shape[3]
    result = lax.dot_general(
        home.reshape(-1, width_x), sx, (((1,), (1,)), ((), ())), precision=lax.Precision.HIGH
    )
    return result.reshape(velocity.shape)


def solution(mesh):
    fine = Mesh(mesh.devices.reshape(SIZES), AXES)
    spec = P(None, ("x", "yhi", "core"), ("z", "ylo"), None)
    return jax.shard_map(
        on_device,
        mesh=fine,
        in_specs=(spec, P(), P(), P(), P(), P(), P()),
        out_specs=spec,
        check_vma=False,
    )
```

```python
import functools

import jax
import jax.numpy as jnp
import numpy as np
from jax import lax
from jax.experimental import pallas as pl
from jax.experimental.pallas import tpu as pltpu
from jax.sharding import Mesh
from jax.sharding import PartitionSpec as P

AXES = ("z", "ylo", "x", "yhi", "core")
SIZES = (8, 2, 4, 2, 2)
MESH = pl.DeviceIdType.MESH
HIGHEST = lax.Precision.HIGHEST
F32 = jnp.float32
BLK = 32
NBY, NBZ, NBX = 8, 4, 8
ORDER = (1, 2, 0)
SIDE = 9.0 / 20.0
STENCIL = (63.0 / 80.0, 9.0 / 100.0, -7.0 / 1200.0)


def tridiagonal_tables(side, count):
    piv, cp = np.zeros(count), np.zeros(count)
    before = 0.0
    for i in range(count):
        piv[i] = 1.0 / (1.0 - side * before)
        before = cp[i] = side * piv[i]
    first, last = np.zeros(count), np.zeros(count)
    first[0] = cp[0]
    for i in range(1, count):
        first[i] = -cp[i] * first[i - 1]
    last[-1] = cp[-1]
    for i in range(count - 2, -1, -1):
        first[i] -= cp[i] * first[i + 1]
        last[i] = -cp[i] * last[i + 1]
    return np.stack([piv, cp, first, last])


def reduced_inverse(table, blocks):
    first, last = table[2], table[3]
    full = np.eye(16)
    for i in range(blocks):
        before, after = 8 + (i - 1) % blocks, (i + 1) % blocks
        full[i, before] += first[0]
        full[i, after] += last[0]
        full[8 + i, before] += first[-1]
        full[8 + i, after] += last[-1]
    return np.linalg.inv(full)


def pade_off_diagonal(count):
    left = np.eye(count) + SIDE * (np.roll(np.eye(count), 1, 1) + np.roll(np.eye(count), -1, 1))
    right = sum(
        w * (np.roll(np.eye(count), k + 1, 1) - np.roll(np.eye(count), -k - 1, 1))
        for k, w in enumerate(STENCIL)
    )
    return float(np.linalg.solve(left, right)[0, 1])


def outside_profile():
    inner = 122
    matrix = np.eye(inner) + SIDE * (np.eye(inner, k=1) + np.eye(inner, k=-1))
    profile = np.zeros((8, 128))
    for e, row in enumerate((0, 1, 2, 125, 126, 127)):
        profile[e, row] = 1.0
    unit = np.zeros(inner)
    unit[0] = -SIDE
    profile[2, 3:125] = np.linalg.solve(matrix, unit)
    profile[3, 3:125] = np.linalg.solve(matrix, unit[::-1])
    return profile


def iota(shape, dim):
    return lax.broadcasted_iota(jnp.int32, shape, dim)


def wrapped_offset(shape, first_row, count):
    offset = iota(shape, 1) - iota(shape, 0) - first_row
    return jnp.where(offset < 0, offset + count, offset)


def metric_rows(matrix_ref, first_row, count, unit):
    block = matrix_ref[pl.ds(first_row, BLK), :]
    offset = wrapped_offset(block.shape, first_row, count)
    weight = jnp.where(offset == 1, 0.5 / unit, jnp.where(offset == count - 1, -0.5 / unit, 0.0))
    return jnp.broadcast_to(jnp.sum(block * weight, axis=1, keepdims=True), (BLK, 128))


def filter_slack(matrix_ref, count):
    shape = (count, count)
    offset = wrapped_offset(shape, 0, count)
    change = matrix_ref[...] - jnp.where(offset == 0, 1.0, 0.0)
    around = 0.5 * (pltpu.roll(change, 1, 0) + pltpu.roll(change, count - 1, 0))
    sixth = jnp.zeros(shape, F32)
    for k, w in enumerate((-20.0, 15.0, -6.0, 1.0)):
        sixth = jnp.where((offset == k) | (offset == (count - k) % count), w / 64.0, sixth)
    basis = sixth + around
    top = jnp.sum((change + around) * basis, axis=1, keepdims=True)
    return top / jnp.sum(basis * basis, axis=1, keepdims=True)


def block_tables(slack_ref, all_ref):
    def side(i):
        return 0.5 - 0.5 * slack_ref[pl.ds(i, 8, stride=BLK), :]

    def forward(i, carry):
        before, first = carry
        a = side(i)
        piv = 1.0 / (1.0 - a * before)
        cp = a * piv
        first = jnp.where(i == 0, cp, -cp * first)
        all_ref[0, i] = piv
        all_ref[1, i] = cp
        all_ref[2, i] = first
        return cp, first

    zero = jnp.zeros((8, 128), F32)
    lax.fori_loop(0, BLK, forward, (zero, zero))

    def backward(k, carry):
        first, last = carry
        i = BLK - 1 - k
        cp = all_ref[1, i]
        first = all_ref[2, i] - cp * first
        last = jnp.where(k == 0, cp, -cp * last)
        all_ref[2, i] = first
        all_ref[3, i] = last
        return first, last

    lax.fori_loop(0, BLK, backward, (zero, zero))


def invert_reduced(all_ref, blocks):
    sub, lane = iota((8, 128), 0), iota((8, 128), 1)
    before = 8 + jnp.where(sub == 0, blocks - 1, sub - 1)
    after = jnp.where(sub == blocks - 1, 0, sub + 1)
    valid = sub < blocks

    def rows(own, first, last):
        value = jnp.where(lane == own, 1.0, 0.0)
        value += jnp.where(valid & (lane == before), first, 0.0)
        return value + jnp.where(valid & (lane == after), last, 0.0)

    full = jnp.concatenate(
        [
            rows(sub, all_ref[2, 0], all_ref[3, 0]),
            rows(8 + sub, all_ref[2, BLK - 1], all_ref[3, BLK - 1]),
        ],
        axis=0,
    )
    sub, lane = iota((16, 128), 0), iota((16, 128), 1)
    full += jnp.where(lane == 16 + sub, 1.0, 0.0)

    def eliminate(k, full):
        column = jnp.sum(jnp.where(lane == k, full, 0.0), axis=1, keepdims=True)
        row = jnp.sum(jnp.where(sub == k, full, 0.0), axis=0, keepdims=True)
        pivot = jnp.sum(jnp.where(sub == k, column, 0.0), axis=0, keepdims=True)[:, :1]
        row = row / pivot
        return jnp.where(sub == k, row, full - column * row)

    return lax.fori_loop(0, 16, eliminate, full)


def loop(count, body, carry, unroll=8):
    steps = count // unroll

    def several(k, carry):
        for j in range(unroll):
            carry = body(k * unroll + j, carry)
        return carry

    carry = lax.fori_loop(0, steps, several, carry)
    for i in range(steps * unroll, count):
        carry = body(i, carry)
    return carry


def each(count, body, unroll=8):
    def step(i, carry):
        body(i)
        return carry

    loop(count, step, 0, unroll)


def halves(value):
    high = value.astype(jnp.bfloat16)
    return high, (value - high.astype(F32)).astype(jnp.bfloat16)


def contract(a, b, dims):
    return lax.dot_general(a, b, (dims, ((), ())), preferred_element_type=F32)


def solve_lines(rhs, table_ref, out_ref):
    def forward(i, before):
        value = rhs(i) * table_ref[0, pl.ds(i, 1), :] - table_ref[1, pl.ds(i, 1), :] * before
        out_ref[i] = value
        return value

    last = loop(BLK, forward, jnp.zeros((BLK, 128), F32))

    def backward(k, after):
        i = BLK - 2 - k
        value = out_ref[i] - table_ref[1, pl.ds(i, 1), :] * after
        out_ref[i] = value
        return value

    loop(BLK - 1, backward, last)


def derivative_rhs(field):
    def rhs(i):
        total = STENCIL[0] * (field[i + 4] - field[i + 2])
        total += STENCIL[1] * (field[i + 5] - field[i + 1])
        return total + STENCIL[2] * (field[i + 6] - field[i])

    return rhs


def filter_rhs(field, slack_ref, first_row):
    def rhs(i):
        total = (field[i] + field[i + 6]) - 6.0 * (field[i + 1] + field[i + 5])
        total += 15.0 * (field[i + 2] + field[i + 4]) - 20.0 * field[i + 3]
        return total * (slack_ref[pl.ds(first_row + i, 1), :] * (1.0 / 64.0))

    return rhs


def kernel(
    u_hbm,
    dx,
    dy_hbm,
    dz_hbm,
    sy_hbm,
    sz_hbm,
    const_hbm,
    sx_hbm,
    result,
    home,
    sx,
    sx_high,
    sx_low,
    u,
    dy,
    dz,
    sy,
    sz,
    const,
    uz,
    uy,
    prod,
    gz,
    gy,
    w0,
    wz,
    vz,
    qy,
    vy,
    turned,
    out,
    edge,
    fix,
    es,
    er,
    dxb,
    dtop,
    dbot,
    inner,
    outer,
    slack_y,
    slack_z,
    all_y,
    all_z,
    tab_d,
    tab_y,
    tab_z,
    met_y,
    met_z,
    rdy,
    rdz,
    rsy,
    rsz,
    ze,
    ye,
    dma,
    loc,
    tin_s,
    tin_r,
    es_s,
    es_r,
    halo_s,
    halo_r,
    ze_s,
    ze_r,
    ye_s,
    ye_r,
    tout_s,
    tout_r,
    edge_s,
    edge_r,
):
    z, x = lax.axis_index("z"), lax.axis_index("x")
    ylo, yhi, core = lax.axis_index("ylo"), lax.axis_index("yhi"), lax.axis_index("core")
    me = (yhi * 2 + ylo) * 2 + core
    first_y = pl.multiple_of(z * BLK, BLK)
    first_z = pl.multiple_of(x * BLK, BLK)
    started = []

    def flip(index, bit):
        return 1 - index if bit else index

    def partner(k):
        return {"yhi": flip(yhi, k >> 2), "ylo": flip(ylo, (k >> 1) & 1), "core": flip(core, k & 1)}

    def number(d):
        return (d["yhi"] * 2 + d["ylo"]) * 2 + d["core"]

    def x_lanes(g):
        return pl.ds(pl.multiple_of(g * 128, 128), 128)

    def z_rows(d):
        return pl.multiple_of((d["yhi"] * 2 + d["core"]) * 8, 8)

    def y_rows(d):
        return pl.multiple_of(d["ylo"] * 16, 16)

    def lines(i):
        return pl.ds(i, 1)

    here = {"yhi": yhi, "ylo": ylo, "core": core}
    remote = functools.partial(pltpu.make_async_remote_copy, device_id_type=MESH)

    def start(copy):
        copy.start()
        started.append(copy)

    greeted = [partner(k) for k in range(1, 8)]
    greeted += [{"x": lax.rem(x + k, NBZ)} for k in range(1, NBZ)]
    greeted += [{"z": lax.rem(z + k, NBY)} for k in range(1, NBY)]
    barrier = pltpu.get_barrier_semaphore()
    for d in greeted:
        pl.semaphore_signal(barrier, inc=1, device_id=d, device_id_type=MESH)

    first_x = pl.multiple_of(me * 128, 128)
    loads = [
        pltpu.make_async_copy(dx.at[pl.ds(first_x, 128), pl.ds(first_x, 128)], dxb, dma.at[0])
    ]
    for b in range(NBX):
        loads.append(
            pltpu.make_async_copy(dx.at[pl.ds(b * 128, 8), :], dtop.at[b], dma.at[1 + b])
        )
        loads.append(
            pltpu.make_async_copy(dx.at[pl.ds(b * 128 + 120, 8), :], dbot.at[b], dma.at[9 + b])
        )
    pairs = ((u_hbm, u), (const_hbm, const), (dy_hbm, dy), (dz_hbm, dz), (sy_hbm, sy), (sz_hbm, sz), (sx_hbm, sx))
    for i, (src, dst) in enumerate(pairs):
        loads.append(pltpu.make_async_copy(src, dst, dma.at[17 + i]))
    for load in loads:
        load.start()

    pl.semaphore_wait(barrier, len(greeted))

    def exchange_in(c, k):
        d = partner(k)
        return remote(
            src_ref=u_hbm.at[c, :, :, x_lanes(number(d))],
            dst_ref=uz.at[c, pl.ds(3 + z_rows(here), 8), pl.ds(y_rows(here), 16), :],
            send_sem=tin_s.at[c, k],
            recv_sem=tin_r.at[c, k],
            device_id=d,
        )

    def keep_in(c):
        return pltpu.make_async_copy(
            u_hbm.at[c, :, :, x_lanes(me)],
            uz.at[c, pl.ds(3 + z_rows(here), 8), pl.ds(y_rows(here), 16), :],
            loc.at[c],
        )

    far_first = (4, 5, 2, 6, 3, 7, 1)

    def begin():
        for c in ORDER[:2]:
            for k in far_first:
                exchange_in(c, k).start()
            keep_in(c).start()

    def begin_last():
        keep_in(ORDER[2]).start()
        for k in far_first:
            for c in ORDER[:2]:
                exchange_in(c, k).wait_send()
            start(exchange_in(ORDER[2], k))

    def exchange_extra(k):
        d = partner(k)
        return remote(
            src_ref=es.at[number(d)],
            dst_ref=er.at[me],
            send_sem=es_s.at[k],
            recv_sem=es_r.at[k],
            device_id=d,
        )

    def extras():
        for load in loads:
            load.wait()
        column_block = iota((8, 1024), 1) // 128
        picked = []
        for b in range(NBX):
            rows = jnp.concatenate([dtop[b, 0:3], dbot[b, 5:8], jnp.zeros((2, 1024), F32)], axis=0)
            picked.append(jnp.where(column_block == b, 0.0, rows))
        high, low = halves(jnp.concatenate(picked, axis=0))
        both = jnp.concatenate([high, low], axis=0)
        for c in range(3):
            p_high, p_low = halves((u[c] * u[0]).reshape(128, 1024))
            value = contract(both, p_high, ((1,), (1,)))
            value = value[:64] + value[64:] + contract(high, p_low, ((1,), (1,)))
            es[:, c] = value.reshape(NBX, 8, 128)
        for k in range(1, 8):
            start(exchange_extra(k))
        er[me] = es[me]

    def spread(full, first, out_ref):
        lane = iota(full.shape, 1)

        def one(k):
            column = jnp.sum(jnp.where(lane == first + k, full, 0.0), axis=1, keepdims=True)
            out_ref[k] = jnp.broadcast_to(column, full.shape)

        each(out_ref.shape[0], one, 4)

    def derivative_tables():
        spread(const[0:16, :], 0, rdy)
        spread(const[16:32, :], 0, rdz)
        spread(const[32:64, :], 0, tab_d)
        met_y[...] = metric_rows(dy, first_y, 256, pade_off_diagonal(256)) * 0.1
        met_z[...] = metric_rows(dz, first_z, 128, pade_off_diagonal(128)) * 0.1

    def split_filter():
        def part(i):
            rows = pl.ds(i * 16, 16)
            sx_high[rows, :], sx_low[rows, :] = halves(sx[rows, :])

        each(64, part, 2)

    def x_tables():
        unit_x = pade_off_diagonal(1024)
        row, col = iota((128, 128), 0), iota((128, 128), 1)
        ends = jnp.where((row == 0) | (row == 127), 1.0 / unit_x, 0.5 / unit_x)
        weight = jnp.where(col == row + 1, ends, jnp.where(col == row - 1, -ends, 0.0))
        metric = lax.dot_general(
            jnp.ones((8, 128), F32),
            dxb[...] * weight,
            (((1,), (1,)), ((), ())),
            precision=HIGHEST,
            preferred_element_type=F32,
        )
        lane, sub = iota((8, 128), 1), iota((8, 128), 0)

        def metric_at(i):
            return jnp.sum(jnp.where(lane == i, metric, 0.0), axis=1, keepdims=True)

        single = (lane < 3) | (lane > 124)
        at_end = jnp.where(sub == 2, metric_at(2), metric_at(125))
        profile = const[64:72, :] * jnp.where(single, 1.0, metric / at_end)
        high, low = halves(profile)
        outer[...] = jnp.concatenate([high, high, low, jnp.zeros_like(low)], axis=0)
        high, low = halves(dxb[...].T)
        inner[0:128, 0:128] = high
        inner[128:256, 0:128] = high
        inner[0:128, 128:256] = low
        inner[128:256, 128:256] = jnp.zeros_like(low)

    def filter_tables():
        slack_y[...] = jnp.broadcast_to(filter_slack(sy, 256), (256, 128))
        half = jnp.broadcast_to(filter_slack(sz, 128), (128, 128))
        slack_z[0:128, :] = half
        slack_z[128:256, :] = half
        block_tables(slack_y, all_y)
        block_tables(slack_z, all_z)

        def pick(i):
            for t in range(4):
                tab_y[t, lines(i), :] = all_y[t, i, pl.ds(z, 1), :]
                tab_z[t, lines(i), :] = all_z[t, i, pl.ds(x, 1), :]

        each(BLK, pick, 4)
        spread(invert_reduced(all_y, NBY), 16, rsy)
        spread(invert_reduced(all_z, NBZ), 16, rsz)

    def halo(stage, c, side):
        field, axis, size = ((uz, "x", NBZ), (uy, "z", NBY), (wz, "x", NBZ), (qy, "z", NBY))[stage]
        index = {"z": z, "x": x}[axis]
        if side == 0:
            src, dst, to = 32, 0, lax.rem(index + 1, size)
        else:
            src, dst, to = 3, 35, lax.rem(index + size - 1, size)
        return remote(
            src_ref=field.at[c, pl.ds(src, 3)],
            dst_ref=field.at[c, pl.ds(dst, 3)],
            send_sem=halo_s.at[stage, c, side],
            recv_sem=halo_r.at[stage, c, side],
            device_id={axis: to},
        )

    def start_halo(stage, c):
        for side in range(2):
            start(halo(stage, c, side))

    def wait_halo(stage, c):
        for side in range(2):
            halo(stage, c, side).wait_recv()

    def end_copy(axis, op, c, k):
        buf, send, recv = {"x": (ze, ze_s, ze_r), "z": (ye, ye_s, ye_r)}[axis]
        index, size = {"x": (x, NBZ), "z": (z, NBY)}[axis]
        return remote(
            src_ref=buf.at[op, c, index],
            dst_ref=buf.at[op, c, index],
            send_sem=send.at[op, c, k],
            recv_sem=recv.at[op, c, k],
            device_id={axis: lax.rem(index + k, size)},
        )

    def start_ends(axis, op, c, solved):
        buf, index, size = {"x": (ze, x, NBZ), "z": (ye, z, NBY)}[axis]
        buf[op, c, index, 0] = solved[c, 0]
        buf[op, c, index, 1] = solved[c, BLK - 1]
        for k in sorted(range(1, size), key=lambda k: -min(k, size - k)):
            start(end_copy(axis, op, c, k))

    def neighbours(axis, op, c, inverse):
        buf, index, size = {"x": (ze, x, NBZ), "z": (ye, z, NBY)}[axis]
        for k in range(1, size):
            end_copy(axis, op, c, k).wait_recv()
        values = []
        for target in (8 + lax.rem(index + size - 1, size), lax.rem(index + 1, size)):
            total = None
            for j in range(size):
                for end in range(2):
                    term = inverse[8 * end + j, lines(target), :] * buf[op, c, j, end]
                    total = term if total is None else total + term
            values.append(total)
        return values

    def turn(src, dst, first):
        flat = src.reshape(src.shape[0] * BLK, 128)

        def one(i):
            dst[first[1] + i] = flat[pl.ds(first[0] * BLK + i, BLK, stride=BLK), :]

        each(BLK, one)

    def minus_ends(value, table, i, before, after):
        return value - table[2, lines(i), :] * before - table[3, lines(i), :] * after

    def arrive(c):
        for k in range(1, 8):
            exchange_in(c, k).wait_recv()
        keep_in(c).wait()
        start_halo(0, c)
        turn(uz.at[c], uy.at[c], (3, 3))
        start_halo(1, c)

    def slope_y(c):
        wait_halo(1, c)

        def multiply(i):
            prod[i] = uy[c, i] * uy[1, i]

        each(38, multiply)
        solve_lines(derivative_rhs(prod), tab_d, gy.at[c])
        start_ends("z", 0, c, gy)

    def slope_z(c):
        wait_halo(0, c)

        def multiply(i):
            prod[i] = uz[c, i] * uz[2, i]

        each(38, multiply)
        solve_lines(derivative_rhs(prod), tab_d, gz.at[c])
        start_ends("x", 0, c, gz)

    def slope_x(c):
        if c == ORDER[0]:
            for k in range(1, 8):
                exchange_extra(k).wait_recv()

        def part(q, carry):
            rows = pl.ds(3 + 8 * q, 8)
            velocity = uz[c, rows]
            high, low = halves((velocity * uz[0, rows]).reshape(256, 128))
            value = contract(jnp.concatenate([high, low], axis=1), inner[...], ((1,), (0,)))
            total = (value[:, :128] + value[:, 128:]).reshape(8, BLK, 128)
            outside = []
            for low_y in range(2):
                source = ((q // 2) * 2 + low_y) * 2 + lax.rem(q, 2)
                high, low = halves(er[source, c])
                given = jnp.concatenate([high, low, high, jnp.zeros_like(low)], axis=0)
                value = contract(given, outer[...], ((0,), (0,)))
                outside.append(value.reshape(8, 16, 128))
            total += jnp.concatenate(outside, axis=1)
            w0[c, pl.ds(8 * q, 8)] = velocity - 0.1 * total
            return carry

        lax.fori_loop(0, 4, part, 0)

    def advance(c):
        before, after = neighbours("z", 0, c, rdy)

        def correct_y(i):
            gy[c, i] = met_y[lines(i), :] * minus_ends(gy[c, i], tab_d, i, before, after)

        each(BLK, correct_y)
        turn(gy.at[c], turned, (0, 0))
        before_z, after_z = neighbours("x", 0, c, rdz)

        def correct_z(i):
            slope = met_z[lines(i), :] * minus_ends(gz[c, i], tab_d, i, before_z, after_z)
            wz[c, 3 + i] = w0[c, i] - slope - turned[i]

        each(BLK, correct_z)
        start_halo(2, c)

    def smooth_z(c):
        wait_halo(2, c)
        solve_lines(filter_rhs(wz.at[c], slack_z, first_z), tab_z, vz.at[c])
        start_ends("x", 1, c, vz)

    def smoothed_z(c):
        before, after = neighbours("x", 1, c, rsz)

        def one(i):
            turned[i] = wz[c, 3 + i] + minus_ends(vz[c, i], tab_z, i, before, after)

        each(BLK, one)
        turn(turned, qy.at[c], (0, 3))
        start_halo(3, c)

    def exchange_out(c, k):
        d = partner(k)
        return remote(
            src_ref=out.at[c, pl.ds(z_rows(d), 8), pl.ds(y_rows(d), 16), :],
            dst_ref=home.at[c, :, :, x_lanes(me)],
            send_sem=tout_s.at[c, k],
            recv_sem=tout_r.at[c, k],
            device_id=d,
        )

    def keep_out(c):
        return pltpu.make_async_copy(
            out.at[c, pl.ds(z_rows(here), 8), pl.ds(y_rows(here), 16), :],
            home.at[c, :, :, x_lanes(me)],
            loc.at[3 + c],
        )

    def smooth_y(c):
        wait_halo(3, c)
        solve_lines(filter_rhs(qy.at[c], slack_y, first_y), tab_y, vy.at[c])
        start_ends("z", 1, c, vy)

        def one(i):
            turned[i] = qy[c, 3 + i] + vy[c, i]

        each(BLK, one)
        turn(turned, out.at[c], (0, 0))
        for k in far_first:
            start(exchange_out(c, k))
        keep_out(c).start()

    def edge_copy(c, k):
        d = partner(k)
        return remote(
            src_ref=edge.at[c, :, pl.ds(z_rows(d), 8), :],
            dst_ref=fix.at[c, :, :, x_lanes(me)],
            send_sem=edge_s.at[c, k],
            recv_sem=edge_r.at[c, k],
            device_id=d,
        )

    def correct(c):
        before, after = neighbours("z", 1, c, rsy)
        edge[c, 0] = before
        edge[c, 1] = after
        for k in far_first:
            start(edge_copy(c, k))
        fix[c, :, :, x_lanes(me)] = edge[c, :, pl.ds(z_rows(here), 8), :]

    def leave(c):
        for k in range(1, 8):
            exchange_out(c, k).wait_recv()
        keep_out(c).wait()
        for k in range(1, 8):
            edge_copy(c, k).wait_recv()
        first = tab_y[2, pl.ds(y_rows(here), 16), :]
        last = tab_y[3, pl.ds(y_rows(here), 16), :]

        def one(g):
            lanes = x_lanes(g)
            before, after = fix[c, 0, :, lanes], fix[c, 1, :, lanes]
            for i in range(8):
                value = home[c, i, :, lanes] - first * before[i : i + 1]
                home[c, i, :, lanes] = value - last * after[i : i + 1]

        each(8, one, 2)
        high, low = halves(home[c].reshape(128, 1024))
        both = jnp.concatenate([high, low], axis=0)

        def filter_x(j):
            lanes = pl.ds(pl.multiple_of(j * 256, 256), 256)
            value = contract(both, sx_high[lanes, :], ((1,), (1,)))
            value = value[:128] + value[128:] + contract(high, sx_low[lanes, :], ((1,), (1,)))
            result[c, :, :, lanes] = value.reshape(8, 16, 256)

        each(4, filter_x, 1)

    one, two, three = ORDER
    steps = [
        (begin,),
        (extras,),
        (derivative_tables,),
        (x_tables,),
        (filter_tables,),
        (split_filter,),
        (begin_last,),
        (arrive, one),
        (arrive, two),
        (slope_y, one),
        (slope_y, two),
        (slope_z, two),
        (slope_z, one),
        (arrive, three),
        (slope_x, one),
        (advance, one),
        (slope_y, three),
        (slope_z, three),
        (slope_x, two),
        (advance, two),
        (smooth_z, one),
        (slope_x, three),
        (smooth_z, two),
        (smoothed_z, one),
        (advance, three),
        (smoothed_z, two),
        (smooth_y, one),
        (smooth_z, three),
        (smooth_y, two),
        (smoothed_z, three),
        (correct, one),
        (smooth_y, three),
        (correct, two),
        (leave, one),
        (correct, three),
        (leave, two),
        (leave, three),
    ]
    for step in steps[:STOP]:
        step[0](*step[1:])
    for copy in started:
        copy.wait_send()


STOP = 99


def on_device(velocity, dx, dy, dz, sx, sy, sz):
    table = tridiagonal_tables(SIDE, BLK)
    const = np.zeros((72, 128), np.float32)
    const[0:16, :16] = reduced_inverse(table, NBY)
    const[16:32, :16] = reduced_inverse(table, NBZ)
    const[32:64, :4] = table.T
    const[64:72] = outside_profile()
    vmem = pl.BlockSpec(memory_space=pltpu.VMEM)
    big, wide, one = (3, BLK, BLK, 128), (3, BLK + 6, BLK, 128), (BLK, BLK, 128)
    shapes = (
        velocity.shape, (256, 256), (128, 128), (256, 256), (128, 128), (72, 128),
        wide, wide, (BLK + 6, BLK, 128), big, big, big, wide, big, wide, big, one, big,
        (3, 2, BLK, 128), (3, 2, 8, 1024),
        (NBX, 3, 8, 128), (NBX, 3, 8, 128), (128, 128), (NBX, 8, 1024), (NBX, 8, 1024),
    )
    scratch = [pltpu.VMEM(velocity.shape, F32), pltpu.VMEM((1024, 1024), F32)]
    scratch += [pltpu.VMEM((1024, 1024), jnp.bfloat16)] * 2
    scratch += [pltpu.VMEM(s, F32) for s in shapes]
    scratch += [pltpu.VMEM((256, 256), jnp.bfloat16), pltpu.VMEM((32, 128), jnp.bfloat16)]
    shapes = (
        (256, 128), (256, 128), (4, BLK, 8, 128), (4, BLK, 8, 128),
        (4, BLK, 128), (4, BLK, 128), (4, BLK, 128), (BLK, 128), (BLK, 128),
        (16, 16, 128), (16, 16, 128), (16, 16, 128), (16, 16, 128),
        (2, 3, NBZ, 2, BLK, 128), (2, 3, NBY, 2, BLK, 128),
    )
    scratch += [pltpu.VMEM(s, F32) for s in shapes]
    counts = (
        (24,), (6,), (3, 8), (3, 8), (8,), (8,), (4, 3, 2), (4, 3, 2),
        (2, 3, NBZ), (2, 3, NBZ), (2, 3, NBY), (2, 3, NBY), (3, 8), (3, 8),
        (3, 8), (3, 8),
    )
    scratch += [pltpu.SemaphoreType.DMA(s) for s in counts]
    return pl.pallas_call(
        kernel,
        out_shape=jax.ShapeDtypeStruct(velocity.shape, F32),
        in_specs=[pl.BlockSpec(memory_space=pl.ANY)] * 8,
        out_specs=vmem,
        scratch_shapes=scratch,
        compiler_params=pltpu.CompilerParams(
            collective_id=1, has_side_effects=True, vmem_limit_bytes=60 * 1024 * 1024
        ),
        name="blocks",
    )(velocity, dx, dy, dz, sy, sz, jnp.asarray(const), sx)


def solution(mesh):
    fine = Mesh(mesh.devices.reshape(SIZES), AXES)
    spec = P(None, ("x", "yhi", "core"), ("z", "ylo"), None)
    return jax.shard_map(
        on_device,
        mesh=fine,
        in_specs=(spec, P(), P(), P(), P(), P(), P()),
        out_specs=spec,
        check_vma=False,
    )
```
